256 devices in a mesh: pop: 64 (over y, x_hi, z), merge: 4 (over x_lo, core).
Axes of the slice: x: 4 (x_hi: 2, x_lo: 2; x = x_hi * 2 + x_lo), y: 4, z: 8, core: 2. Of those that a mesh axis runs over, the one named last changes fastest.
Arguments:
- slab: float32 [256, 256, 4096], P('pop', 'merge'), may hold values from -6 to 6
- sample_counts: int32 [2], replicated, may hold values from 160 to 255
- mode_rows_one: float32 [96, 256], replicated, may hold values from -0.375 to 0.375
- mode_rows_two: float32 [96, 256], replicated, may hold values from -0.375 to 0.375
- merge_tensor: float32 [96, 96, 96], replicated, may hold values from -0.0625 to 0.0625
- ancestral_modes: float32 [96, 256], replicated, may hold values from -0.625 to 0.625
Outputs:
- merged: float32 [4096, 256], P(('pop', 'merge'))
The draws below stay inside these ranges and needn't reach their ends.
All inputs are finite; a program needn't handle non-finite values.
Results may differ from the reference program's by a relative error of at most 0.000076.
Values sent between devices are 32-bit elements; how exact they have to be, the bound alone decides.
A program may use at most 64 MiB of HBM per device.

```python
import jax
import jax.numpy as jnp
from jax import lax

N1 = 256
N2 = 256
NA = 256
K = 96
COLS = 4096


def level_of(key, shape, split, low, top_value):
    factor_of, own = 1.0, jax.random.fold_in(key, 6)
    for position, shards_of in split:
        draws = jnp.exp(jax.random.uniform(jax.random.fold_in(own, position), (shards_of,), jnp.float32, low / len(split), top_value / len(split)))
        factor_of = factor_of * jnp.repeat(draws, shape[position] // shards_of).reshape([-1 if axis == position else 1 for axis in range(len(shape))])
    return factor_of


def normal_values(key, dims, scale, limit, pieces=(), held_as=jnp.bfloat16):
    result = jax.random.normal(key, dims, jnp.float32) * scale
    if len(pieces) > 0:
        result = level_of(key, dims, pieces, -0.22, 0.18) * result
    return jnp.clip(result, min=-limit, max=limit).astype(held_as)


def setup_inputs(seed: int = 0) -> dict:
    splits = jax.random.split(jax.random.key(seed), 7)
    return {
        "slab": normal_values(splits[0], (N1, N2, COLS), 1.0, 6.0, ((0, 64), (1, 4)), jnp.float32),
        "sample_counts": jax.random.randint(splits[1], (2,), 5 * min(N1, N2) // 8, min(N1, N2)).astype(jnp.int32),
        "mode_rows_one": normal_values(splits[2], (K, N1), N1 ** -0.5, 0.375, (), jnp.float32),
        "mode_rows_two": normal_values(splits[3], (K, N2), N2 ** -0.5, 0.375, (), jnp.float32),
        "merge_tensor": normal_values(splits[4], (K, K, K), (K * K) ** -0.5, 0.0625, (), jnp.float32),
        "ancestral_modes": normal_values(splits[5], (K, NA), K ** -0.5, 0.625, (), jnp.float32),
    }


branch_one = 0.00025
branch_two = 0.0004


def prepared(rows, count, length, branch):
    order = jnp.arange(rows.shape[0], dtype=jnp.float32)
    decay = jnp.exp(-branch * order * (order + 1.0) / 2.0).astype(rows.dtype)
    keep = jnp.arange(length, dtype=jnp.int32) <= count
    return jnp.where(keep[None, :], rows, jnp.zeros_like(rows)) * decay[:, None]


def reference(slab, sample_counts, mode_rows_one, mode_rows_two, merge_tensor, ancestral_modes):
    high = lax.Precision.HIGHEST
    proj_one = prepared(mode_rows_one, sample_counts[0], N1, branch_one)
    proj_two = prepared(mode_rows_two, sample_counts[1], N2, branch_two)
    modal = jnp.einsum("ka,abc->kbc", proj_one, slab, precision=high)
    folded = jnp.einsum("mnj,nb->jmb", merge_tensor, proj_two, precision=high)
    summed = lax.dot_general(modal.reshape(K * N2, COLS), folded.reshape(K, K * N2), (((0,), (1,)), ((), ())), precision=high)
    return jnp.dot(summed, ancestral_modes, precision=high)
```

```python
import jax
import jax.numpy as jnp
from jax import lax
from jax.sharding import PartitionSpec as P

branch_one = 0.00025
branch_two = 0.0004


def prepared(rows, first, count, branch):
    order = jnp.arange(rows.shape[0], dtype=jnp.float32)
    decay = jnp.exp(-branch * order * (order + 1.0) / 2.0)
    keep = first + jnp.arange(rows.shape[1], dtype=jnp.int32) <= count
    return jnp.where(keep[None, :], rows, jnp.zeros_like(rows)) * decay[:, None]


def on_device(slab, sample_counts, mode_rows_one, mode_rows_two, merge_tensor, ancestral_modes):
    high = lax.Precision.HIGHEST
    per_pop, per_merge, cols = slab.shape
    begin_one = lax.axis_index("pop") * per_pop
    begin_two = lax.axis_index("merge") * per_merge
    rows_one = lax.dynamic_slice_in_dim(mode_rows_one, begin_one, per_pop, 1)
    rows_two = lax.dynamic_slice_in_dim(mode_rows_two, begin_two, per_merge, 1)
    proj_one = prepared(rows_one, begin_one, sample_counts[0], branch_one)
    proj_two = prepared(rows_two, begin_two, sample_counts[1], branch_two)
    half = jnp.einsum("ma,mnj->anj", proj_one, merge_tensor, precision=high)
    weights = jnp.einsum("nb,anj->abj", proj_two, half, precision=high)
    partial = lax.dot_general(
        slab, weights, (((0, 1), (0, 1)), ((), ())), precision=lax.Precision.HIGH
    )
    summed = lax.psum_scatter(partial, ("pop", "merge"), scatter_dimension=0, tiled=True)
    return jnp.dot(summed, ancestral_modes, precision=high)


def solution(mesh):
    in_specs = (P("pop", "merge", None), P(), P(), P(), P(), P())
    out_specs = P(("pop", "merge"), None)
    return jax.shard_map(
        on_device, mesh=mesh, in_specs=in_specs, out_specs=out_specs, check_vma=False
    )
```

```python
import jax
import jax.numpy as jnp
from jax import lax
from jax.experimental import pallas as pl
from jax.experimental.pallas import tpu as pltpu
from jax.sharding import PartitionSpec as P

branch_one = 0.00025
branch_two = 0.0004
MESH = pl.DeviceIdType.MESH
HIGH = lax.Precision.HIGHEST
LAG = 4
F32 = jnp.float32


def device(y, xh, z, xl, c):
    return ((y * 2 + xh) * 8 + z, xl * 2 + c)


def flip(bit, by):
    return (bit + by) % 2


def prepared(rows, count, branch):
    order = lax.broadcasted_iota(jnp.int32, rows.shape, 0).astype(F32)
    entry = lax.broadcasted_iota(jnp.int32, rows.shape, 1)
    decay = jnp.exp(-branch * order * (order + 1.0) / 2.0)
    return jnp.where(entry <= count, rows, 0.0) * decay


def kernel(
    slab, counts, rows_one, rows_two, merge, ancestral, out,
    slab_v, one_v, two_v, merge_v, anc_v, anc_pad, one_b, half_v, weights, whi, part, from_core,
    arrived_y, arrived_x, tiles_out, pieces,
    load_sem, slab_sem, merge_sem, core_send, core_recv, y_send, y_recv, x_send, x_recv,
    final_send, final_recv,
):
    pop, mrg = lax.axis_index("pop"), lax.axis_index("merge")
    z = pop % 8
    xh = (pop // 8) % 2
    y = pop // 16
    xl, c = mrg // 2, mrg % 2
    yh, yl = y // 2, y % 2
    zh, zl = z // 2, z % 2
    low = 1 - z // 4

    def y_target(i):
        k = (i % 4 + 1) % 4
        return k, flip(yh, k // 2) * 2 + flip(yl, k % 2), flip(xh, 1 - i // 4)

    def x_target(i):
        k = i % 4
        xr = 1 - k % 2
        u = (i // 4) * 2 + k // 2
        return u, flip(yh, 1 - i // 4) * 2 + flip(yl, k // 2), xr

    def slab_copy(i, h):
        if h == 0:
            _, ty, tx = y_target(i)
            pair = ty * 4 + tx * 2
        else:
            _, ty, xr = x_target(i)
            pair = ty * 4 + flip(xh, xr) * 2 + 1
        begin = pl.multiple_of(pair * 256, 256)
        return pltpu.make_async_copy(
            slab.at[:, :, pl.ds(begin, 256)], slab_v.at[i, h], slab_sem.at[i, h]
        )

    load_one = pltpu.make_async_copy(rows_one, one_v, load_sem.at[0])
    load_two = pltpu.make_async_copy(rows_two, two_v, load_sem.at[1])
    load_anc = pltpu.make_async_copy(ancestral, anc_v, load_sem.at[2])
    load_one.start()
    load_two.start()
    merge_loads = [
        pltpu.make_async_copy(
            merge.at[:, pl.ds(b * 4, 4)], merge_v.at[:, pl.ds(b * 4, 4)], merge_sem.at[b]
        )
        for b in range(3)
    ]
    for load in merge_loads:
        load.start()

    def start_slab(i, _):
        slab_copy(i, 0).start()
        slab_copy(i, 1).start()
        return 0

    lax.fori_loop(0, 8, start_slab, 0)
    load_anc.start()

    barrier = pltpu.get_barrier_semaphore()

    def tell(dev):
        pl.semaphore_signal(barrier, inc=1, device_id=dev, device_id_type=MESH)

    tell(device(y, xh, z, xl, 1 - c))
    for k in range(1, 4):
        tell(device(flip(yh, k // 2) * 2 + flip(yl, k % 2), xh, z, xl, c))
        tell(device(y, flip(xh, k // 2), z, flip(xl, k % 2), c))

    def tell_sources(i, _):
        n, zs = i // 8, i % 8
        ys = low * y + (1 - low) * n
        xhs = low * (n // 2) + (1 - low) * xh
        xls = low * (n % 2) + (1 - low) * (zh - 2)
        me = (ys == y) & (xhs == xh) & (xls == xl) & (zs == z)

        @pl.when(jnp.logical_not(me))
        def _():
            tell(device(ys, xhs, zs, xls, c))

        return 0

    lax.fori_loop(0, 32, tell_sources, 0)
    own_piece = (low == 1) | (zh == 2 + xl)

    load_one.wait()
    load_two.wait()
    one = prepared(one_v[...], counts[0], branch_one)
    entry = lax.broadcasted_iota(jnp.int32, one.shape, 1)
    for a in range(4):
        column = jnp.sum(jnp.where(entry == pop * 4 + a, one, 0.0), axis=1, keepdims=True)
        one_b[a] = jnp.broadcast_to(column[:, :, None], (96, 8, 96))
    two = prepared(two_v[...], counts[1], branch_two)
    two = pltpu.roll(two, (256 - mrg * 64) % 256, 1)
    two_t = jnp.transpose(two[:, :128])[:64]
    half_v[...] = jnp.zeros_like(half_v)
    for b in range(3):
        merge_loads[b].wait()

        def mode_step(mb, acc):
            for s in range(8):
                m = mb * 8 + s
                block = merge_v[m, b * 4 : b * 4 + 4]
                acc = tuple(acc[a] + one_b[a, m][None] * block for a in range(4))
            return acc

        acc = lax.fori_loop(0, 12, mode_step, tuple(jnp.zeros((4, 8, 96), F32) for _ in range(4)))
        for a in range(4):
            half_v[b * 32 : b * 32 + 32, a * 128 : a * 128 + 96] = acc[a].reshape(32, 96)
    wide = jnp.dot(two_t, half_v[...], precision=HIGH, preferred_element_type=F32)
    flat = jnp.concatenate([wide[:, a * 128 : a * 128 + 128] for a in range(4)], axis=0)
    w = jnp.transpose(flat)[:96]
    w_hi = w.astype(jnp.bfloat16)
    weights[:96] = w_hi
    weights[96:] = (w - w_hi.astype(F32)).astype(jnp.bfloat16)
    whi[...] = w_hi

    pl.semaphore_wait(barrier, jnp.where(own_piece, 38, 39))

    def core_copy(i, h):
        return pltpu.make_async_remote_copy(
            src_ref=part.at[i, h, 1 - c],
            dst_ref=from_core.at[i, h],
            send_sem=core_send,
            recv_sem=core_recv.at[i, h],
            device_id=device(y, xh, z, xl, 1 - c),
            device_id_type=MESH,
        )

    def contract(i, h):
        slab_copy(i, h).wait()
        x = slab_v[i, h].reshape(256, 256)
        x_hi = x.astype(jnp.bfloat16)
        x_lo = (x - x_hi.astype(F32)).astype(jnp.bfloat16)
        both = jnp.dot(weights[...], x_hi, preferred_element_type=F32)
        rest = jnp.dot(whi[...], x_lo, preferred_element_type=F32)
        total = both[:96] + both[96:] + rest
        for j in range(2):
            for t in range(2):
                part[i, h, j, t] = total[j * 48 : j * 48 + 48, t * 128 : t * 128 + 128]
        core_copy(i, h).start()

    def forward(i):
        k, ty, _ = y_target(i)
        core_copy(i, 0).wait_recv()
        part[i, 0, c] = part[i, 0, c] + from_core[i, 0]

        @pl.when(k > 0)
        def _():
            pltpu.make_async_remote_copy(
                src_ref=part.at[i, 0, c],
                dst_ref=arrived_y.at[k - 1, i // 4],
                send_sem=y_send,
                recv_sem=y_recv.at[k - 1, i // 4],
                device_id=device(ty, xh, z, xl, c),
                device_id_type=MESH,
            ).start()

        u, _, xr = x_target(i)
        core_copy(i, 1).wait_recv()
        part[i, 1, c] = part[i, 1, c] + from_core[i, 1]

        def send_x(tr):
            t = flip(xl, tr)
            pltpu.make_async_remote_copy(
                src_ref=part.at[i, 1, c, t],
                dst_ref=arrived_x.at[xr * 2 + tr - 1, u],
                send_sem=x_send,
                recv_sem=x_recv.at[xr * 2 + tr - 1, u],
                device_id=device(y, flip(xh, xr), z, t, c),
                device_id_type=MESH,
            ).start()

        send_x(1)

        @pl.when(xr == 1)
        def _():
            send_x(0)

    def step(i, _):
        @pl.when(i < 8)
        def _():
            contract(i, 0)
            contract(i, 1)

        @pl.when(i >= LAG)
        def _():
            forward(i - LAG)

        return 0

    lax.fori_loop(0, 8 + LAG, step, 0)

    load_anc.wait()
    anc_pad[...] = jnp.zeros_like(anc_pad)
    anc_pad[0:48] = anc_v[0:48]
    anc_pad[64:112] = anc_v[48:96]

    def spread(total, n, h):
        zero = jnp.zeros((16, 128), F32)
        stacked = jnp.concatenate([total, zero, pltpu.roll(total, 120, 1), zero], axis=0)
        turned = jnp.transpose(stacked)
        for g in range(8):
            tiles_out[h, n, g] = turned[g * 16 : g * 16 + 8]

    def final_copy(n, h, g, slot, dev):
        return pltpu.make_async_remote_copy(
            src_ref=tiles_out.at[h, n, g],
            dst_ref=pieces.at[slot],
            send_sem=final_send,
            recv_sem=final_recv,
            device_id=dev,
            device_id_type=MESH,
        )

    def owner_step(n, _):
        q, t = n // 2, n % 2
        @pl.when(t == 0)
        def _():
            for k in range(3):
                pltpu.make_async_copy(
                    arrived_y.at[k, q], arrived_y.at[k, q], y_recv.at[k, q]
                ).wait()

        mine = part[q * 4 + 3, 0, c, t]
        spread(mine + arrived_y[0, q, t] + arrived_y[1, q, t] + arrived_y[2, q, t], n, 0)
        slot = (xh * 2 + xl) * 16 + z * 2 + c
        for r in range(8):
            gz, gx, gc = flip(zl, r // 4), flip(xl, r // 2 % 2), flip(c, r % 2)
            g = gz * 4 + gx * 2 + gc
            dev = device(y, flip(xh, 1 - q), t * 2 + gz, gx, gc)
            if r == 0:
                own = (q == 1) & (zh == t)

                @pl.when(own)
                def _():
                    pieces[slot] = tiles_out[0, n, g]

                @pl.when(jnp.logical_not(own))
                def _():
                    final_copy(n, 0, g, slot, dev).start()
            else:
                final_copy(n, 0, g, slot, dev).start()

        for k in range(3):
            pltpu.make_async_copy(
                arrived_x.at[k, n], arrived_x.at[k, n], x_recv.at[k, n]
            ).wait()
        mine = part[q * 4 + t * 2 + 1, 1, c, xl]
        spread(mine + arrived_x[0, n] + arrived_x[1, n] + arrived_x[2, n], n, 1)
        slot = y * 16 + z * 2 + c
        ty = flip(yh, 1 - q) * 2 + flip(yl, t)
        for r in range(8):
            gz, gx, gc = flip(zl, r // 4), flip(xl, r // 2 % 2), flip(c, r % 2)
            g = gz * 4 + gx * 2 + gc
            dev = device(ty, xh, (2 + xl) * 2 + gz, gx, gc)
            if r == 0:
                own = (n == 2) & (zh == 2 + xl)

                @pl.when(own)
                def _():
                    pieces[slot] = tiles_out[1, n, g]

                @pl.when(jnp.logical_not(own))
                def _():
                    final_copy(n, 1, g, slot, dev).start()
            else:
                final_copy(n, 1, g, slot, dev).start()
        return 0

    lax.fori_loop(0, 4, owner_step, 0)

    def drain(ref, sem):
        pltpu.make_async_copy(ref, ref, sem).wait()

    def drain_pieces(sem):
        @pl.when(own_piece)
        def _():
            drain(pieces.at[pl.ds(0, 63)], sem)

        @pl.when(jnp.logical_not(own_piece))
        def _():
            drain(pieces, sem)

    drain_pieces(final_recv)

    def add(i, acc):
        return acc[0] + pieces[i * 2], acc[1] + pieces[i * 2 + 1]

    first, second = lax.fori_loop(1, 32, add, (pieces[0], pieces[1]), unroll=True)
    lane = lax.broadcasted_iota(jnp.int32, (8, 128), 1)
    top = jnp.where(lane < 64, first, pltpu.roll(second, 64, 1))
    bottom = jnp.where(lane < 64, pltpu.roll(first, 64, 1), second)
    out[...] = jnp.dot(
        jnp.concatenate([top, bottom], axis=0), anc_pad[...],
        precision=HIGH, preferred_element_type=F32,
    )

    drain(from_core, core_send)
    drain(arrived_y, y_send)
    drain(arrived_x, x_send)
    drain_pieces(final_send)


def on_device(slab, sample_counts, mode_rows_one, mode_rows_two, merge_tensor, ancestral_modes):
    hbm = pl.BlockSpec(memory_space=pl.ANY)
    dma = pltpu.SemaphoreType.DMA
    return pl.pallas_call(
        kernel,
        out_shape=jax.ShapeDtypeStruct((16, 256), F32),
        in_specs=[hbm, pl.BlockSpec(memory_space=pltpu.SMEM), hbm, hbm, hbm, hbm],
        out_specs=pl.BlockSpec(memory_space=pltpu.VMEM),
        scratch_shapes=[
            pltpu.VMEM((8, 2, 4, 64, 256), F32),
            pltpu.VMEM((96, 256), F32),
            pltpu.VMEM((96, 256), F32),
            pltpu.VMEM((96, 12, 8, 96), F32),
            pltpu.VMEM((96, 256), F32),
            pltpu.VMEM((128, 256), F32),
            pltpu.VMEM((4, 96, 8, 96), F32),
            pltpu.VMEM((96, 512), F32),
            pltpu.VMEM((192, 256), jnp.bfloat16),
            pltpu.VMEM((96, 256), jnp.bfloat16),
            pltpu.VMEM((8, 2, 2, 2, 48, 128), F32),
            pltpu.VMEM((8, 2, 2, 48, 128), F32),
            pltpu.VMEM((3, 2, 2, 48, 128), F32),
            pltpu.VMEM((3, 4, 48, 128), F32),
            pltpu.VMEM((2, 4, 8, 8, 128), F32),
            pltpu.VMEM((64, 8, 128), F32),
            dma((3,)),
            dma((8, 2)),
            dma((3,)),
            dma,
            dma((8, 2)),
            dma,
            dma((3, 2)),
            dma,
            dma((3, 4)),
            dma,
            dma,
        ],
        compiler_params=pltpu.CompilerParams(
            collective_id=0, has_side_effects=True, vmem_limit_bytes=56 << 20
        ),
    )(
        slab,
        sample_counts,
        mode_rows_one,
        mode_rows_two,
        merge_tensor.reshape(96, 12, 8, 96),
        ancestral_modes,
    )


def solution(mesh):
    in_specs = (P("pop", "merge", None), P(), P(), P(), P(), P())
    out_specs = P(("pop", "merge"), None)
    return jax.shard_map(
        on_device, mesh=mesh, in_specs=in_specs, out_specs=out_specs, check_vma=False
    )
```

```python
import jax
import jax.numpy as jnp
from jax import lax
from jax.experimental import pallas as pl
from jax.experimental.pallas import tpu as pltpu
from jax.sharding import PartitionSpec as P

branch_one = 0.00025
branch_two = 0.0004
MESH = pl.DeviceIdType.MESH
HIGH = lax.Precision.HIGHEST
F32 = jnp.float32


def device(y, xh, z, xl, c):
    return ((y * 2 + xh) * 8 + z, xl * 2 + c)


def prepared(rows, count, branch):
    order = lax.broadcasted_iota(jnp.int32, rows.shape, 0).astype(F32)
    entry = lax.broadcasted_iota(jnp.int32, rows.shape, 1)
    decay = jnp.exp(-branch * order * (order + 1.0) / 2.0)
    return jnp.where(entry <= count, rows, 0.0) * decay


def kernel(
    slab, counts, rows_one, rows_two, merge, ancestral, out,
    slab_v, one_v, two_v, merge_v, anc_v, anc_pad, one_b, half_v, weights, whi, part, from_core,
    arrived_y, arrived_x, tiles_out, pieces, stack,
    load_sem, slab_sem, merge_sem, core_send, core_recv, y_send, y_recv, x_send, x_recv,
    final_send, final_recv, entered,
):
    pop, mrg = lax.axis_index("pop"), lax.axis_index("merge")
    z = pop % 8
    xh = (pop // 8) % 2
    y = pop // 16
    xl, c = mrg // 2, mrg % 2
    zh = z // 2
    bits_yh, bits_yl = (y // 2, 1 - y // 2), (y % 2, 1 - y % 2)
    bits_xh, bits_xl = (xh, 1 - xh), (xl, 1 - xl)
    bits_zl, bits_c = (z % 2, 1 - z % 2), (c, 1 - c)
    ys = [bits_yh[k // 2] * 2 + bits_yl[k % 2] for k in range(4)]

    barrier = pltpu.get_barrier_semaphore()

    def tell(sem, dev):
        pl.semaphore_signal(sem, inc=1, device_id=dev, device_id_type=MESH)

    for k in (4, 3, 5, 2, 6, 1, 7):
        tell(barrier, device(y, xh, (z + k) % 8, xl, c))
    for k in (2, 3, 1):
        tell(barrier, device(ys[k], xh, z, xl, 1 - c))
        tell(barrier, device(y, bits_xh[k // 2], z, bits_xl[k % 2], 1 - c))
    tell(barrier, device(y, xh, z, 1 - xl, c))
    tell(barrier, device(y, xh, z, xl, 1 - c))

    def y_target(i):
        k = (i % 4 + 1) % 4
        return k, ys[k], bits_xh[1 - i // 4]

    def x_target(i):
        k = i % 4
        xr = 1 - k % 2
        u = (i // 4) * 2 + k // 2
        return u, bits_yh[1 - i // 4] * 2 + bits_yl[k // 2], xr

    def slab_copy(i, h):
        if h == 0:
            _, ty, tx = y_target(i)
            pair = ty * 4 + tx * 2
        else:
            _, ty, xr = x_target(i)
            pair = ty * 4 + bits_xh[xr] * 2 + 1
        begin = pl.multiple_of(pair * 256, 256)
        return pltpu.make_async_copy(
            slab.at[:, :, pl.ds(begin, 256)],
            slab_v.at[i // 2, :, :, pl.ds((i % 2 * 2 + h) * 256, 256)],
            slab_sem.at[i, h],
        )

    load_one = pltpu.make_async_copy(rows_one, one_v, load_sem.at[0])
    load_two = pltpu.make_async_copy(rows_two, two_v, load_sem.at[1])
    load_anc = [
        pltpu.make_async_copy(
            ancestral.at[:, pl.ds(e * 128, 128)], anc_v.at[e], load_sem.at[2 + e]
        )
        for e in range(2)
    ]
    load_one.start()
    load_two.start()
    merge_loads = [
        pltpu.make_async_copy(
            merge.at[:, pl.ds(b * 4, 4)], merge_v.at[:, pl.ds(b * 4, 4)], merge_sem.at[b]
        )
        for b in range(3)
    ]
    for load in merge_loads:
        load.start()

    for i in range(8):
        slab_copy(i, 0).start()
        slab_copy(i, 1).start()
    for load in load_anc:
        load.start()
    own_piece = (z < 4) | (zh == 2 + xl)

    load_one.wait()
    load_two.wait()
    one = prepared(one_v[...], counts[0], branch_one)
    entry = lax.broadcasted_iota(jnp.int32, one.shape, 1)
    for a in range(4):
        column = jnp.sum(jnp.where(entry == pop * 4 + a, one, 0.0), axis=1, keepdims=True)
        one_b[a] = jnp.broadcast_to(column[:, :, None], (96, 8, 96))
    two = prepared(two_v[...], counts[1], branch_two)
    two = pltpu.roll(two, (256 - mrg * 64) % 256, 1)
    two_t = jnp.transpose(two[:, :128])[:64]
    two_hi = two_t.astype(jnp.bfloat16)
    two_lo = (two_t - two_hi.astype(F32)).astype(jnp.bfloat16)
    half_v[...] = jnp.zeros_like(half_v)
    for b in range(3):
        merge_loads[b].wait()

        def mode_step(mb, acc):
            for s in range(8):
                m = mb * 8 + s
                block = merge_v[m, b * 4 : b * 4 + 4]
                acc = tuple(acc[a] + one_b[a, m][None] * block for a in range(4))
            return acc

        acc = lax.fori_loop(0, 12, mode_step, tuple(jnp.zeros((4, 8, 96), F32) for _ in range(4)))
        for a in range(4):
            half_v[b * 32 : b * 32 + 32, a * 128 : a * 128 + 96] = acc[a].reshape(32, 96)
    half = half_v[...]
    half_hi = half.astype(jnp.bfloat16)
    half_lo = (half - half_hi.astype(F32)).astype(jnp.bfloat16)
    wide = (
        jnp.dot(two_hi, half_hi, preferred_element_type=F32)
        + jnp.dot(two_lo, half_hi, preferred_element_type=F32)
        + jnp.dot(two_hi, half_lo, preferred_element_type=F32)
    )
    flat = jnp.concatenate([wide[:, a * 128 : a * 128 + 128] for a in range(4)], axis=0)
    w = jnp.transpose(flat)[:96]
    w_hi = w.astype(jnp.bfloat16)
    weights[:96] = w_hi
    weights[96:] = (w - w_hi.astype(F32)).astype(jnp.bfloat16)
    whi[...] = w_hi

    def core_copy(i, h):
        return pltpu.make_async_remote_copy(
            src_ref=part.at[i, h, 1 - c],
            dst_ref=from_core.at[i, h],
            send_sem=core_send,
            recv_sem=core_recv.at[i, h],
            device_id=device(y, xh, z, xl, 1 - c),
            device_id_type=MESH,
        )

    def contract(b):
        for i in range(2):
            for h in range(2):
                slab_copy(b * 2 + i, h).wait()
        for i in range(2):
            for h in range(2):
                at = (i * 2 + h) * 256
                x = slab_v[b, :, :, at : at + 256].reshape(256, 256)
                x_hi = x.astype(jnp.bfloat16)
                x_lo = (x - x_hi.astype(F32)).astype(jnp.bfloat16)
                both = jnp.dot(weights[...], x_hi, preferred_element_type=F32)
                rest = jnp.dot(whi[...], x_lo, preferred_element_type=F32)
                total = both[:96] + both[96:] + rest
                for j in range(2):
                    for t in range(2):
                        part[b * 2 + i, h, j, t] = total[
                            j * 48 : j * 48 + 48, t * 128 : t * 128 + 128
                        ]

    def swap(b):
        for i in range(2):
            for h in range(2):
                core_copy(b * 2 + i, h).start()

    def forward(i):
        k, ty, _ = y_target(i)
        core_copy(i, 0).wait_recv()
        part[i, 0, c] = part[i, 0, c] + from_core[i, 0]
        pltpu.make_async_remote_copy(
            src_ref=part.at[i, 0, c],
            dst_ref=arrived_y.at[k, i // 4],
            send_sem=y_send,
            recv_sem=y_recv.at[k, i // 4],
            device_id=device(ty, xh, z, xl, 1 - c),
            device_id_type=MESH,
        ).start()

        u, _, xr = x_target(i)
        core_copy(i, 1).wait_recv()
        part[i, 1, c] = part[i, 1, c] + from_core[i, 1]
        for tr in (1, 0):
            pltpu.make_async_remote_copy(
                src_ref=part.at[i, 1, c, bits_xl[tr]],
                dst_ref=arrived_x.at[xr * 2 + tr, u],
                send_sem=x_send,
                recv_sem=x_recv.at[xr * 2 + tr, u],
                device_id=device(y, bits_xh[xr], z, bits_xl[tr], 1 - c),
                device_id_type=MESH,
            ).start()

    contract(0)
    pl.semaphore_wait(barrier, 15)
    tell(entered, device(y, xh, z, 1 - xl, c))
    tell(entered, device(y, xh, z, 1 - xl, 1 - c))
    swap(0)
    contract(1)
    swap(1)
    contract(2)
    swap(2)
    pl.semaphore_wait(entered, 2)
    forward(0)
    forward(1)
    contract(3)
    swap(3)
    for i in range(2, 8):
        forward(i)

    for load in load_anc:
        load.wait()
    anc_pad[...] = jnp.zeros_like(anc_pad)
    stack[...] = jnp.zeros_like(stack)
    for js in range(8):
        for half in range(2):
            at = js * 16 + half * 8
            for e in range(2):
                anc_pad[at : at + 6, e * 128 : e * 128 + 128] = anc_v[
                    e, pl.ds(half * 48 + js, 6, stride=8), :
                ]

    row = lax.broadcasted_iota(jnp.int32, (6, 8, 128), 1)
    group = lax.broadcasted_iota(jnp.int32, (6, 8, 128), 2) // 16

    def spread(total, n, h):
        x = total.reshape(6, 8, 128)
        for b in (1, 2, 4):
            odd_row, odd_group = row // b % 2 == 1, group // b % 2 == 1
            above = pltpu.roll(pltpu.roll(x, 8 - b, 1), 16 * b, 2)
            below = pltpu.roll(pltpu.roll(x, b, 1), 128 - 16 * b, 2)
            x = jnp.where(odd_row == odd_group, x, jnp.where(odd_group, above, below))
        for j in range(6):
            tiles_out[h, n, pl.ds(j, 8, stride=8), :] = x[j]

    def send_pieces(n, h, slot, ty, txh, tzh, own):
        for r in range(8):
            gz, gx, gc = bits_zl[r // 4], bits_xl[r // 2 % 2], bits_c[r % 2]
            begin = pl.multiple_of(gz * 32 + gx * 16 + gc * 8, 8)
            send = pltpu.make_async_remote_copy(
                src_ref=tiles_out.at[h, n, pl.ds(begin, 6), :],
                dst_ref=pieces.at[slot, pl.ds(0, 6), :],
                send_sem=final_send,
                recv_sem=final_recv,
                device_id=device(ty, txh, tzh * 2 + gz, gx, gc),
                device_id_type=MESH,
            )
            if r == 0 and own is not None:

                @pl.when(own)
                def _():
                    pieces[slot, 0:6] = tiles_out[h, n, pl.ds(begin, 6), :]

                @pl.when(jnp.logical_not(own))
                def _():
                    send.start()
            else:
                send.start()

    slot_y = (xh * 2 + xl) * 16 + z * 2 + c
    slot_x = y * 16 + z * 2 + c
    for n in range(4):
        q, t = n // 2, n % 2
        for k in range(4):
            if t == 0:
                pltpu.make_async_copy(
                    arrived_y.at[k, q], arrived_y.at[k, q], y_recv.at[k, q]
                ).wait()
            pltpu.make_async_copy(
                arrived_x.at[k, n], arrived_x.at[k, n], x_recv.at[k, n]
            ).wait()
        spread(
            (arrived_y[0, q, t] + arrived_y[1, q, t]) + (arrived_y[2, q, t] + arrived_y[3, q, t]),
            n,
            0,
        )
        spread((arrived_x[0, n] + arrived_x[1, n]) + (arrived_x[2, n] + arrived_x[3, n]), n, 1)
        send_pieces(n, 0, slot_y, y, bits_xh[1 - q], t, zh == t if q == 1 else None)
        ty = bits_yh[1 - q] * 2 + bits_yl[t]
        send_pieces(n, 1, slot_x, ty, xh, 2 + xl, zh == 2 + xl if n == 2 else None)

    def drain(ref, sem):
        pltpu.make_async_copy(ref, ref, sem).wait()

    def drain_pieces(sem):
        @pl.when(own_piece)
        def _():
            drain(pieces.at[pl.ds(0, 63), pl.ds(0, 6), :], sem)

        @pl.when(jnp.logical_not(own_piece))
        def _():
            drain(pieces.at[:, pl.ds(0, 6), :], sem)

    drain_pieces(final_recv)

    upper, lower = pieces[0, 0:6], pieces[1, 0:6]
    for i in range(1, 32):
        upper = upper + pieces[i * 2, 0:6]
        lower = lower + pieces[i * 2 + 1, 0:6]
    stack[0:6] = lower
    stack[8:14] = upper
    turned = jnp.transpose(stack[...])
    left = turned[0:16]
    for js in range(1, 8):
        left = left + pltpu.roll(turned[js * 16 : js * 16 + 16], js * 16, 1)
    out[...] = jnp.dot(left, anc_pad[...], precision=HIGH, preferred_element_type=F32)

    drain(from_core, core_send)
    drain(arrived_y, y_send)
    drain(arrived_x, x_send)
    drain_pieces(final_send)


def on_device(slab, sample_counts, mode_rows_one, mode_rows_two, merge_tensor, ancestral_modes):
    hbm = pl.BlockSpec(memory_space=pl.ANY)
    dma = pltpu.SemaphoreType.DMA
    return pl.pallas_call(
        kernel,
        out_shape=pltpu.VMEM((16, 256), F32),
        in_specs=[hbm, pl.BlockSpec(memory_space=pltpu.SMEM), hbm, hbm, hbm, hbm],
        out_specs=pl.BlockSpec(memory_space=pltpu.VMEM),
        scratch_shapes=[
            pltpu.VMEM((4, 4, 64, 1024), F32),
            pltpu.VMEM((96, 256), F32),
            pltpu.VMEM((96, 256), F32),
            pltpu.VMEM((96, 12, 8, 96), F32),
            pltpu.VMEM((2, 96, 128), F32),
            pltpu.VMEM((128, 256), F32),
            pltpu.VMEM((4, 96, 8, 96), F32),
            pltpu.VMEM((96, 512), F32),
            pltpu.VMEM((192, 256), jnp.bfloat16),
            pltpu.VMEM((96, 256), jnp.bfloat16),
            pltpu.VMEM((8, 2, 2, 2, 48, 128), F32),
            pltpu.VMEM((8, 2, 2, 48, 128), F32),
            pltpu.VMEM((4, 2, 2, 48, 128), F32),
            pltpu.VMEM((4, 4, 48, 128), F32),
            pltpu.VMEM((2, 4, 64, 128), F32),
            pltpu.VMEM((64, 8, 128), F32),
            pltpu.VMEM((128, 128), F32),
            dma((4,)),
            dma((8, 2)),
            dma((3,)),
            dma,
            dma((8, 2)),
            dma,
            dma((4, 2)),
            dma,
            dma((4, 4)),
            dma,
            dma,
            pltpu.SemaphoreType.REGULAR,
        ],
        compiler_params=pltpu.CompilerParams(
            collective_id=0, has_side_effects=True, vmem_limit_bytes=56 << 20
        ),
    )(
        slab,
        sample_counts,
        mode_rows_one,
        mode_rows_two,
        merge_tensor.reshape(96, 12, 8, 96),
        ancestral_modes,
    )


def solution(mesh):
    in_specs = (P("pop", "merge", None), P(), P(), P(), P(), P())
    out_specs = P(("pop", "merge"), None)
    return jax.shard_map(
        on_device, mesh=mesh, in_specs=in_specs, out_specs=out_specs, check_vma=False
    )
```

```python
import jax
import jax.numpy as jnp
from jax import lax
from jax.experimental import pallas as pl
from jax.experimental.pallas import tpu as pltpu
from jax.sharding import PartitionSpec as P

branch_one = 0.00025
branch_two = 0.0004
MESH = pl.DeviceIdType.MESH
HIGH = lax.Precision.HIGHEST
F32 = jnp.float32


def device(y, xh, z, xl, c):
    return ((y * 2 + xh) * 8 + z, xl * 2 + c)


def prepared(rows, count, branch):
    order = lax.broadcasted_iota(jnp.int32, rows.shape, 0).astype(F32)
    entry = lax.broadcasted_iota(jnp.int32, rows.shape, 1)
    decay = jnp.exp(-branch * order * (order + 1.0) / 2.0)
    return jnp.where(entry <= count, rows, 0.0) * decay


def kernel(
    slab, counts, rows_one, rows_two, merge, ancestral, out,
    slab_v, one_v, two_v, merge_v, anc_v, anc_pad, one_b, half_v, weights, whi, part, from_core,
    arrived_y, arrived_x, tiles_out, pieces, stack,
    load_sem, slab_sem, merge_sem, core_send, core_recv, y_send, y_recv, x_send, x_recv,
    final_send, final_recv, entered,
):
    pop, mrg = lax.axis_index("pop"), lax.axis_index("merge")
    z = pop % 8
    xh = (pop // 8) % 2
    y = pop // 16
    xl, c = mrg // 2, mrg % 2
    zh = z // 2
    bits_yh, bits_yl = (y // 2, 1 - y // 2), (y % 2, 1 - y % 2)
    bits_xh, bits_xl = (xh, 1 - xh), (xl, 1 - xl)
    bits_zl, bits_c = (z % 2, 1 - z % 2), (c, 1 - c)
    ys = [bits_yh[k // 2] * 2 + bits_yl[k % 2] for k in range(4)]

    barrier = pltpu.get_barrier_semaphore()

    def tell(sem, dev):
        pl.semaphore_signal(sem, inc=1, device_id=dev, device_id_type=MESH)

    for k in (4, 3, 5, 2, 6, 1, 7):
        tell(barrier, device(y, xh, (z + k) % 8, xl, c))
    for k in (2, 3, 1):
        tell(barrier, device(ys[k], xh, z, xl, 1 - c))
        tell(barrier, device(y, bits_xh[k // 2], z, bits_xl[k % 2], 1 - c))
    tell(barrier, device(y, xh, z, xl, 1 - c))

    def y_target(i):
        k = (i % 4 + 1) % 4
        return k, ys[k], bits_xh[1 - i // 4]

    def x_target(i):
        k = i % 4
        xr = 1 - k % 2
        u = (i // 4) * 2 + k // 2
        return u, bits_yh[1 - i // 4] * 2 + bits_yl[k // 2], xr

    def slab_copy(i, h):
        if h == 0:
            _, ty, tx = y_target(i)
            pair = ty * 4 + tx * 2
        else:
            _, ty, xr = x_target(i)
            pair = ty * 4 + bits_xh[xr] * 2 + 1
        begin = pl.multiple_of(pair * 256, 256)
        return pltpu.make_async_copy(
            slab.at[:, :, pl.ds(begin, 256)],
            slab_v.at[h * 2 + i // 4, :, :, pl.ds(i % 4 * 256, 256)],
            slab_sem.at[i, h],
        )

    load_one = pltpu.make_async_copy(rows_one, one_v, load_sem.at[0])
    load_two = pltpu.make_async_copy(rows_two, two_v, load_sem.at[1])
    load_anc = [
        pltpu.make_async_copy(
            ancestral.at[:, pl.ds(e * 128, 128)], anc_v.at[e], load_sem.at[2 + e]
        )
        for e in range(2)
    ]
    load_one.start()
    load_two.start()
    merge_loads = [
        pltpu.make_async_copy(
            merge.at[:, pl.ds(b * 4, 4)], merge_v.at[:, pl.ds(b * 4, 4)], merge_sem.at[b]
        )
        for b in range(3)
    ]
    for load in merge_loads:
        load.start()

    for h in range(2):
        for i in range(8):
            slab_copy(i, h).start()
    for load in load_anc:
        load.start()
    own_piece = (z < 4) | (zh == 2 + xl)

    load_one.wait()
    load_two.wait()
    one = prepared(one_v[...], counts[0], branch_one)
    entry = lax.broadcasted_iota(jnp.int32, one.shape, 1)
    for a in range(4):
        column = jnp.sum(jnp.where(entry == pop * 4 + a, one, 0.0), axis=1, keepdims=True)
        one_b[a] = jnp.broadcast_to(column[:, :, None], (96, 8, 96))
    two = prepared(two_v[...], counts[1], branch_two)
    two = pltpu.roll(two, (256 - mrg * 64) % 256, 1)
    two_t = jnp.transpose(two[:, :128])[:64]
    two_hi = two_t.astype(jnp.bfloat16)
    two_lo = (two_t - two_hi.astype(F32)).astype(jnp.bfloat16)
    half_v[...] = jnp.zeros_like(half_v)
    for b in range(3):
        merge_loads[b].wait()

        def mode_step(mb, acc):
            for s in range(8):
                m = mb * 8 + s
                block = merge_v[m, b * 4 : b * 4 + 4]
                acc = tuple(acc[a] + one_b[a, m][None] * block for a in range(4))
            return acc

        acc = lax.fori_loop(0, 12, mode_step, tuple(jnp.zeros((4, 8, 96), F32) for _ in range(4)))
        for a in range(4):
            half_v[b * 32 : b * 32 + 32, a * 128 : a * 128 + 96] = acc[a].reshape(32, 96)
    half = half_v[...]
    half_hi = half.astype(jnp.bfloat16)
    half_lo = (half - half_hi.astype(F32)).astype(jnp.bfloat16)
    wide = (
        jnp.dot(two_hi, half_hi, preferred_element_type=F32)
        + jnp.dot(two_lo, half_hi, preferred_element_type=F32)
        + jnp.dot(two_hi, half_lo, preferred_element_type=F32)
    )
    flat = jnp.concatenate([wide[:, a * 128 : a * 128 + 128] for a in range(4)], axis=0)
    w = jnp.transpose(flat)[:96]
    w_hi = w.astype(jnp.bfloat16)
    weights[:96] = w_hi
    weights[96:] = (w - w_hi.astype(F32)).astype(jnp.bfloat16)
    whi[...] = w_hi

    def core_copy(i, h):
        return pltpu.make_async_remote_copy(
            src_ref=part.at[i, h, 1 - c],
            dst_ref=from_core.at[i, h],
            send_sem=core_send,
            recv_sem=core_recv.at[i, h],
            device_id=device(y, xh, z, xl, 1 - c),
            device_id_type=MESH,
        )

    def contract(b):
        h, first = b // 2, b % 2 * 4
        for i in range(4):
            slab_copy(first + i, h).wait()
        for i in range(4):
            x = slab_v[b, :, :, i * 256 : i * 256 + 256].reshape(256, 256)
            x_hi = x.astype(jnp.bfloat16)
            x_lo = (x - x_hi.astype(F32)).astype(jnp.bfloat16)
            both = jnp.dot(weights[...], x_hi, preferred_element_type=F32)
            rest = jnp.dot(whi[...], x_lo, preferred_element_type=F32)
            total = both[:96] + both[96:] + rest
            for j in range(2):
                for t in range(2):
                    part[first + i, h, j, t] = total[
                        j * 48 : j * 48 + 48, t * 128 : t * 128 + 128
                    ]

    def swap(b):
        for i in range(4):
            core_copy(b % 2 * 4 + i, b // 2).start()

    def settle(i, h):
        core_copy(i, h).wait_recv()
        part[i, h, c] = part[i, h, c] + from_core[i, h]

    def send_y(i, t):
        k, ty, _ = y_target(i)
        pltpu.make_async_remote_copy(
            src_ref=part.at[i, 0, c, t],
            dst_ref=arrived_y.at[k, i // 4, t],
            send_sem=y_send,
            recv_sem=y_recv.at[k, i // 4, t],
            device_id=device(ty, xh, z, xl, 1 - c),
            device_id_type=MESH,
        ).start()

    def send_x(i):
        u, _, xr = x_target(i)
        for tr in (1, 0):
            pltpu.make_async_remote_copy(
                src_ref=part.at[i, 1, c, bits_xl[tr]],
                dst_ref=arrived_x.at[xr * 2 + tr, u],
                send_sem=x_send,
                recv_sem=x_recv.at[xr * 2 + tr, u],
                device_id=device(y, bits_xh[xr], z, bits_xl[tr], 1 - c),
                device_id_type=MESH,
            ).start()

    contract(0)
    pl.semaphore_wait(barrier, 14)
    swap(0)
    contract(1)
    swap(1)
    contract(2)
    swap(2)
    for i in range(8):
        settle(i, 0)
        if i == 0:
            for k in (2, 3, 1):
                tell(entered, device(y, bits_xh[k // 2], z, bits_xl[k % 2], 1 - c))
        send_y(i, 0)
    pl.semaphore_wait(entered, 3)
    for i in range(8):
        send_y(i, 1)
    contract(3)
    swap(3)
    for i in range(8):
        settle(i, 1)
        send_x(i)

    for load in load_anc:
        load.wait()
    anc_pad[...] = jnp.zeros_like(anc_pad)
    stack[...] = jnp.zeros_like(stack)
    for js in range(8):
        for half in range(2):
            at = js * 16 + half * 8
            for e in range(2):
                anc_pad[at : at + 6, e * 128 : e * 128 + 128] = anc_v[
                    e, pl.ds(half * 48 + js, 6, stride=8), :
                ]

    row = lax.broadcasted_iota(jnp.int32, (6, 8, 128), 1)
    group = lax.broadcasted_iota(jnp.int32, (6, 8, 128), 2) // 16

    def spread(total, n, h):
        x = total.reshape(6, 8, 128)
        for b in (1, 2, 4):
            odd_row, odd_group = row // b % 2 == 1, group // b % 2 == 1
            above = pltpu.roll(pltpu.roll(x, 8 - b, 1), 16 * b, 2)
            below = pltpu.roll(pltpu.roll(x, b, 1), 128 - 16 * b, 2)
            x = jnp.where(odd_row == odd_group, x, jnp.where(odd_group, above, below))
        for j in range(6):
            tiles_out[h, n, pl.ds(j, 8, stride=8), :] = x[j]

    def send_pieces(n, h, slot, ty, txh, tzh, own, near):
        for r in range(8):
            gz, gx, gc = near + r // 4 * (1 - 2 * near), bits_xl[r // 2 % 2], bits_c[r % 2]
            begin = pl.multiple_of(gz * 32 + gx * 16 + gc * 8, 8)
            send = pltpu.make_async_remote_copy(
                src_ref=tiles_out.at[h, n, pl.ds(begin, 6), :],
                dst_ref=pieces.at[slot, pl.ds(0, 6), :],
                send_sem=final_send,
                recv_sem=final_recv,
                device_id=device(ty, txh, tzh * 2 + gz, gx, gc),
                device_id_type=MESH,
            )
            if r % 4 == 0 and own is not None:
                mine = own & (z % 2 == gz)

                @pl.when(mine)
                def _():
                    pieces[slot, 0:6] = tiles_out[h, n, pl.ds(begin, 6), :]

                @pl.when(jnp.logical_not(mine))
                def _():
                    send.start()
            else:
                send.start()

    slot_y = (xh * 2 + xl) * 16 + z * 2 + c
    slot_x = y * 16 + z * 2 + c
    for n in (0, 2, 1, 3):
        q, t = n // 2, n % 2
        for k in range(4):
            pltpu.make_async_copy(
                arrived_y.at[k, q, t], arrived_y.at[k, q, t], y_recv.at[k, q, t]
            ).wait()
        spread(
            (arrived_y[0, q, t] + arrived_y[1, q, t]) + (arrived_y[2, q, t] + arrived_y[3, q, t]),
            n,
            0,
        )
        send_pieces(n, 0, slot_y, y, bits_xh[1 - q], t, zh == t if q == 1 else None, t)
    for n in range(4):
        q, t = n // 2, n % 2
        for k in range(4):
            pltpu.make_async_copy(
                arrived_x.at[k, n], arrived_x.at[k, n], x_recv.at[k, n]
            ).wait()
        spread((arrived_x[0, n] + arrived_x[1, n]) + (arrived_x[2, n] + arrived_x[3, n]), n, 1)
        ty = bits_yh[1 - q] * 2 + bits_yl[t]
        send_pieces(n, 1, slot_x, ty, xh, 2 + xl, zh == 2 + xl if n == 2 else None, 0)

    def drain(ref, sem):
        pltpu.make_async_copy(ref, ref, sem).wait()

    def drain_pieces(sem):
        @pl.when(own_piece)
        def _():
            drain(pieces.at[pl.ds(0, 63), pl.ds(0, 6), :], sem)

        @pl.when(jnp.logical_not(own_piece))
        def _():
            drain(pieces.at[:, pl.ds(0, 6), :], sem)

    drain_pieces(final_recv)

    upper, lower = pieces[0, 0:6], pieces[1, 0:6]
    for i in range(1, 32):
        upper = upper + pieces[i * 2, 0:6]
        lower = lower + pieces[i * 2 + 1, 0:6]
    stack[0:6] = lower
    stack[8:14] = upper
    turned = jnp.transpose(stack[...])
    left = turned[0:16]
    for js in range(1, 8):
        left = left + pltpu.roll(turned[js * 16 : js * 16 + 16], js * 16, 1)
    out[...] = jnp.dot(left, anc_pad[...], precision=HIGH, preferred_element_type=F32)

    drain(from_core, core_send)
    drain(arrived_y, y_send)
    drain(arrived_x, x_send)
    drain_pieces(final_send)


def on_device(slab, sample_counts, mode_rows_one, mode_rows_two, merge_tensor, ancestral_modes):
    hbm = pl.BlockSpec(memory_space=pl.ANY)
    dma = pltpu.SemaphoreType.DMA
    return pl.pallas_call(
        kernel,
        out_shape=pltpu.VMEM((16, 256), F32),
        in_specs=[hbm, pl.BlockSpec(memory_space=pltpu.SMEM), hbm, hbm, hbm, hbm],
        out_specs=pl.BlockSpec(memory_space=pltpu.VMEM),
        scratch_shapes=[
            pltpu.VMEM((4, 4, 64, 1024), F32),
            pltpu.VMEM((96, 256), F32),
            pltpu.VMEM((96, 256), F32),
            pltpu.VMEM((96, 12, 8, 96), F32),
            pltpu.VMEM((2, 96, 128), F32),
            pltpu.VMEM((128, 256), F32),
            pltpu.VMEM((4, 96, 8, 96), F32),
            pltpu.VMEM((96, 512), F32),
            pltpu.VMEM((192, 256), jnp.bfloat16),
            pltpu.VMEM((96, 256), jnp.bfloat16),
            pltpu.VMEM((8, 2, 2, 2, 48, 128), F32),
            pltpu.VMEM((8, 2, 2, 48, 128), F32),
            pltpu.VMEM((4, 2, 2, 48, 128), F32),
            pltpu.VMEM((4, 4, 48, 128), F32),
            pltpu.VMEM((2, 4, 64, 128), F32),
            pltpu.VMEM((64, 8, 128), F32),
            pltpu.VMEM((128, 128), F32),
            dma((4,)),
            dma((8, 2)),
            dma((3,)),
            dma,
            dma((8, 2)),
            dma,
            dma((4, 2, 2)),
            dma,
            dma((4, 4)),
            dma,
            dma,
            pltpu.SemaphoreType.REGULAR,
        ],
        compiler_params=pltpu.CompilerParams(
            collective_id=0, has_side_effects=True, vmem_limit_bytes=56 << 20
        ),
    )(
        slab,
        sample_counts,
        mode_rows_one,
        mode_rows_two,
        merge_tensor.reshape(96, 12, 8, 96),
        ancestral_modes,
    )


def solution(mesh):
    in_specs = (P("pop", "merge", None), P(), P(), P(), P(), P())
    out_specs = P(("pop", "merge"), None)
    return jax.shard_map(
        on_device, mesh=mesh, in_specs=in_specs, out_specs=out_specs, check_vma=False
    )
```

```python
import jax
import jax.numpy as jnp
from jax import lax
from jax.experimental import pallas as pl
from jax.experimental.pallas import tpu as pltpu
from jax.sharding import PartitionSpec as P

branch_one = 0.00025
branch_two = 0.0004
MESH = pl.DeviceIdType.MESH
HIGH = lax.Precision.HIGHEST
F32 = jnp.float32


def device(y, xh, z, xl, c):
    return ((y * 2 + xh) * 8 + z, xl * 2 + c)


def prepared(rows, count, branch):
    order = lax.broadcasted_iota(jnp.int32, rows.shape, 0).astype(F32)
    entry = lax.broadcasted_iota(jnp.int32, rows.shape, 1)
    decay = jnp.exp(-branch * order * (order + 1.0) / 2.0)
    return jnp.where(entry <= count, rows, 0.0) * decay


def kernel(
    slab, counts, rows_one, rows_two, merge, ancestral, out,
    slab_v, one_v, two_v, merge_v, anc_v, anc_pad, one_b, half_v, weights, whi, part, from_core,
    arrived_y, arrived_x, tiles_out, pieces, stack,
    load_sem, slab_sem, merge_sem, core_send, core_recv, y_send, y_recv, x_send, x_recv,
    final_send, final_recv, entered_near, entered_far,
):
    pop, mrg = lax.axis_index("pop"), lax.axis_index("merge")
    z = pop % 8
    xh = (pop // 8) % 2
    y = pop // 16
    xl, c = mrg // 2, mrg % 2
    zh = z // 2
    bits_yh, bits_yl = (y // 2, 1 - y // 2), (y % 2, 1 - y % 2)
    bits_xh, bits_xl = (xh, 1 - xh), (xl, 1 - xl)
    bits_zl, bits_c = (z % 2, 1 - z % 2), (c, 1 - c)
    ys = [bits_yh[k // 2] * 2 + bits_yl[k % 2] for k in range(4)]

    barrier = pltpu.get_barrier_semaphore()

    def tell(sem, dev):
        pl.semaphore_signal(sem, inc=1, device_id=dev, device_id_type=MESH)


    def y_target(i):
        return y, i % 4, bits_xh[1 - i // 4]

    def x_target(i):
        k = i % 4
        xr = 1 - k % 2
        u = (i // 4) * 2 + k // 2
        return u, u, xr

    def slab_copy(i, h):
        if h == 0:
            _, ty, tx = y_target(i)
            pair = ty * 4 + tx * 2
        else:
            _, ty, xr = x_target(i)
            pair = ty * 4 + bits_xh[xr] * 2 + 1
        begin = pl.multiple_of(pair * 256, 256)
        return pltpu.make_async_copy(
            slab.at[:, :, pl.ds(begin, 256)],
            slab_v.at[h * 2 + i // 4, :, :, pl.ds(i % 4 * 256, 256)],
            slab_sem.at[i, h],
        )

    load_one = pltpu.make_async_copy(rows_one, one_v, load_sem.at[0])
    load_two = pltpu.make_async_copy(rows_two, two_v, load_sem.at[1])
    load_anc = [
        pltpu.make_async_copy(
            ancestral.at[:, pl.ds(e * 128, 128)], anc_v.at[e], load_sem.at[2 + e]
        )
        for e in range(2)
    ]
    load_one.start()
    load_two.start()
    merge_loads = [
        pltpu.make_async_copy(
            merge.at[:, pl.ds(b * 4, 4)], merge_v.at[:, pl.ds(b * 4, 4)], merge_sem.at[b]
        )
        for b in range(3)
    ]
    for load in merge_loads:
        load.start()

    for k in (4, 3, 5, 2, 6, 1, 7):
        tell(barrier, device(y, xh, (z + k) % 8, xl, c))
    for k in (2, 3, 1):
        tell(barrier, device(ys[k], xh, z, xl, 1 - c))
        for core in range(2):
            tell(barrier, device(y, bits_xh[k // 2], z, bits_xl[k % 2], core))
    tell(barrier, device(y, xh, z, xl, 1 - c))
    for h in range(2):
        for i in range(8):
            slab_copy(i, h).start()
    for load in load_anc:
        load.start()
    own_piece = (z < 4) | (zh == 2 + xl)

    load_one.wait()
    load_two.wait()
    one = prepared(one_v[...], counts[0], branch_one)
    entry = lax.broadcasted_iota(jnp.int32, one.shape, 1)
    for a in range(4):
        column = jnp.sum(jnp.where(entry == pop * 4 + a, one, 0.0), axis=1, keepdims=True)
        one_b[a] = jnp.broadcast_to(column[:, :, None], (96, 8, 96))
    two = prepared(two_v[...], counts[1], branch_two)
    two = pltpu.roll(two, (256 - mrg * 64) % 256, 1)
    two_t = jnp.transpose(two[:, :128])[:64]
    two_hi = two_t.astype(jnp.bfloat16)
    two_lo = (two_t - two_hi.astype(F32)).astype(jnp.bfloat16)
    half_v[...] = jnp.zeros_like(half_v)
    for b in range(3):
        merge_loads[b].wait()

        def mode_step(mb, acc):
            for s in range(8):
                m = mb * 8 + s
                block = merge_v[m, b * 4 : b * 4 + 4]
                acc = tuple(acc[a] + one_b[a, m][None] * block for a in range(4))
            return acc

        acc = lax.fori_loop(0, 12, mode_step, tuple(jnp.zeros((4, 8, 96), F32) for _ in range(4)))
        for a in range(4):
            half_v[b * 32 : b * 32 + 32, a * 128 : a * 128 + 96] = acc[a].reshape(32, 96)
    half = half_v[...]
    half_hi = half.astype(jnp.bfloat16)
    half_lo = (half - half_hi.astype(F32)).astype(jnp.bfloat16)
    wide = (
        jnp.dot(two_hi, half_hi, preferred_element_type=F32)
        + jnp.dot(two_lo, half_hi, preferred_element_type=F32)
        + jnp.dot(two_hi, half_lo, preferred_element_type=F32)
    )
    flat = jnp.concatenate([wide[:, a * 128 : a * 128 + 128] for a in range(4)], axis=0)
    w = jnp.transpose(flat)[:96]
    w_hi = w.astype(jnp.bfloat16)
    weights[:96] = w_hi
    weights[96:] = (w - w_hi.astype(F32)).astype(jnp.bfloat16)
    whi[...] = w_hi

    def core_copy(i, h):
        return pltpu.make_async_remote_copy(
            src_ref=part.at[i, h, 1 - c],
            dst_ref=from_core.at[i, h],
            send_sem=core_send,
            recv_sem=core_recv.at[i, h],
            device_id=device(y, xh, z, xl, 1 - c),
            device_id_type=MESH,
        )

    def contract_pair(b, i):
        h, at = b // 2, b % 2 * 4 + i
        x = slab_v[b, :, :, i * 256 : i * 256 + 256].reshape(256, 256)
        x_hi = x.astype(jnp.bfloat16)
        x_lo = (x - x_hi.astype(F32)).astype(jnp.bfloat16)
        both = jnp.dot(weights[...], x_hi, preferred_element_type=F32)
        rest = jnp.dot(whi[...], x_lo, preferred_element_type=F32)
        total = both[:96] + both[96:] + rest
        for j in range(2):
            for t in range(2):
                part[at, h, j, t] = total[j * 48 : j * 48 + 48, t * 128 : t * 128 + 128]

    def arrive(b):
        for i in range(4):
            slab_copy(b % 2 * 4 + i, b // 2).wait()

    def contract(b):
        arrive(b)
        for i in range(4):
            contract_pair(b, i)

    def swap(b):
        for i in range(4):
            core_copy(b % 2 * 4 + i, b // 2).start()

    def settle(i, h):
        core_copy(i, h).wait_recv()
        part[i, h, c] = part[i, h, c] + from_core[i, h]

    def send_y(i, t):
        k, ty, _ = y_target(i)
        pltpu.make_async_remote_copy(
            src_ref=part.at[i, 0, c, t],
            dst_ref=arrived_y.at[k, i // 4, t],
            send_sem=y_send,
            recv_sem=y_recv.at[k, i // 4, t],
            device_id=device(ty, xh, z, xl, 1 - c),
            device_id_type=MESH,
        ).start()

    def send_x(i):
        u, _, xr = x_target(i)
        for tr in (1, 0):
            pltpu.make_async_remote_copy(
                src_ref=part.at[i, 1, c, bits_xl[tr]],
                dst_ref=arrived_x.at[xr * 2 + tr, u],
                send_sem=x_send,
                recv_sem=x_recv.at[xr * 2 + tr, u],
                device_id=device(y, bits_xh[xr], z, bits_xl[tr], 1 - c),
                device_id_type=MESH,
            ).start()

    arrive(0)
    contract_pair(0, 0)
    pl.semaphore_wait(barrier, 17)
    for core in range(2):
        tell(entered_near, device(y, xh, z, 1 - xl, core))
    for k in (2, 3):
        for core in range(2):
            tell(entered_far, device(y, 1 - xh, z, bits_xl[k % 2], core))
    core_copy(0, 0).start()
    for i in range(1, 4):
        contract_pair(0, i)
        core_copy(i, 0).start()
    contract(1)
    swap(1)
    for i in range(8):
        settle(i, 0)
        if i == 4:
            pl.semaphore_wait(entered_near, 2)
        send_y(i, 0)
    contract(2)
    swap(2)
    contract(3)
    swap(3)
    for i in range(4):
        settle(i, 1)
        send_x(i)
    for i in range(8):
        send_y(i, 1)
    for i in range(4, 8):
        settle(i, 1)
        send_x(i)
    pl.semaphore_wait(entered_far, 4)

    for load in load_anc:
        load.wait()
    anc_pad[...] = jnp.zeros_like(anc_pad)
    stack[...] = jnp.zeros_like(stack)
    for js in range(8):
        for half in range(2):
            at = js * 16 + half * 8
            for e in range(2):
                anc_pad[at : at + 6, e * 128 : e * 128 + 128] = anc_v[
                    e, pl.ds(half * 48 + js, 6, stride=8), :
                ]

    row = lax.broadcasted_iota(jnp.int32, (6, 8, 128), 1)
    group = lax.broadcasted_iota(jnp.int32, (6, 8, 128), 2) // 16

    def spread(total, n, h):
        x = total.reshape(6, 8, 128)
        for b in (1, 2, 4):
            odd_row, odd_group = row // b % 2 == 1, group // b % 2 == 1
            above = pltpu.roll(pltpu.roll(x, 8 - b, 1), 16 * b, 2)
            below = pltpu.roll(pltpu.roll(x, b, 1), 128 - 16 * b, 2)
            x = jnp.where(odd_row == odd_group, x, jnp.where(odd_group, above, below))
        for j in range(6):
            tiles_out[h, n, pl.ds(j, 8, stride=8), :] = x[j]

    def send_pieces(n, h, slot, ty, txh, tzh, own, near):
        for r in range(8):
            gz, gx, gc = near + r // 4 * (1 - 2 * near), bits_xl[r // 2 % 2], bits_c[r % 2]
            begin = pl.multiple_of(gz * 32 + gx * 16 + gc * 8, 8)
            send = pltpu.make_async_remote_copy(
                src_ref=tiles_out.at[h, n, pl.ds(begin, 6), :],
                dst_ref=pieces.at[slot, pl.ds(0, 6), :],
                send_sem=final_send,
                recv_sem=final_recv,
                device_id=device(ty, txh, tzh * 2 + gz, gx, gc),
                device_id_type=MESH,
            )
            if r % 4 == 0 and own is not None:
                mine = own & (z % 2 == gz)

                @pl.when(mine)
                def _():
                    pieces[slot, 0:6] = tiles_out[h, n, pl.ds(begin, 6), :]

                @pl.when(jnp.logical_not(mine))
                def _():
                    send.start()
            else:
                send.start()

    slot_y = (xh * 2 + xl) * 16 + z * 2 + c
    slot_x = y * 16 + z * 2 + c
    def deliver_y(n):
        q, t = n // 2, n % 2
        for k in range(4):
            pltpu.make_async_copy(
                arrived_y.at[k, q, t], arrived_y.at[k, q, t], y_recv.at[k, q, t]
            ).wait()
        spread(
            (arrived_y[0, q, t] + arrived_y[1, q, t]) + (arrived_y[2, q, t] + arrived_y[3, q, t]),
            n,
            0,
        )
        send_pieces(n, 0, slot_y, y, bits_xh[1 - q], t, zh == t if q == 1 else None, t)

    def deliver_x(n):
        q, t = n // 2, n % 2
        for k in range(4):
            pltpu.make_async_copy(
                arrived_x.at[k, n], arrived_x.at[k, n], x_recv.at[k, n]
            ).wait()
        spread((arrived_x[0, n] + arrived_x[1, n]) + (arrived_x[2, n] + arrived_x[3, n]), n, 1)
        send_pieces(n, 1, slot_x, n, xh, 2 + xl, (zh == 2 + xl) & (y == n), 0)

    deliver_y(0)
    deliver_y(2)
    deliver_y(1)
    deliver_y(3)
    deliver_x(0)
    deliver_x(1)
    deliver_x(2)
    deliver_x(3)

    def drain(ref, sem):
        pltpu.make_async_copy(ref, ref, sem).wait()

    def drain_pieces(sem):
        @pl.when(own_piece)
        def _():
            drain(pieces.at[pl.ds(0, 63), pl.ds(0, 6), :], sem)

        @pl.when(jnp.logical_not(own_piece))
        def _():
            drain(pieces.at[:, pl.ds(0, 6), :], sem)

    drain_pieces(final_recv)

    upper, lower = pieces[0, 0:6], pieces[1, 0:6]
    for i in range(1, 32):
        upper = upper + pieces[i * 2, 0:6]
        lower = lower + pieces[i * 2 + 1, 0:6]
    stack[0:6] = lower
    stack[8:14] = upper
    turned = jnp.transpose(stack[...])
    left = turned[0:16]
    for js in range(1, 8):
        left = left + pltpu.roll(turned[js * 16 : js * 16 + 16], js * 16, 1)
    out[...] = jnp.dot(left, anc_pad[...], precision=HIGH, preferred_element_type=F32)

    drain(from_core, core_send)
    drain(arrived_y, y_send)
    drain(arrived_x, x_send)
    drain_pieces(final_send)


def on_device(slab, sample_counts, mode_rows_one, mode_rows_two, merge_tensor, ancestral_modes):
    hbm = pl.BlockSpec(memory_space=pl.ANY)
    dma = pltpu.SemaphoreType.DMA
    return pl.pallas_call(
        kernel,
        out_shape=pltpu.VMEM((16, 256), F32),
        in_specs=[hbm, pl.BlockSpec(memory_space=pltpu.SMEM), hbm, hbm, hbm, hbm],
        out_specs=pl.BlockSpec(memory_space=pltpu.VMEM),
        scratch_shapes=[
            pltpu.VMEM((4, 4, 64, 1024), F32),
            pltpu.VMEM((96, 256), F32),
            pltpu.VMEM((96, 256), F32),
            pltpu.VMEM((96, 12, 8, 96), F32),
            pltpu.VMEM((2, 96, 128), F32),
            pltpu.VMEM((128, 256), F32),
            pltpu.VMEM((4, 96, 8, 96), F32),
            pltpu.VMEM((96, 512), F32),
            pltpu.VMEM((192, 256), jnp.bfloat16),
            pltpu.VMEM((96, 256), jnp.bfloat16),
            pltpu.VMEM((8, 2, 2, 2, 48, 128), F32),
            pltpu.VMEM((8, 2, 2, 48, 128), F32),
            pltpu.VMEM((4, 2, 2, 48, 128), F32),
            pltpu.VMEM((4, 4, 48, 128), F32),
            pltpu.VMEM((2, 4, 64, 128), F32),
            pltpu.VMEM((64, 8, 128), F32),
            pltpu.VMEM((128, 128), F32),
            dma((4,)),
            dma((8, 2)),
            dma((3,)),
            dma,
            dma((8, 2)),
            dma,
            dma((4, 2, 2)),
            dma,
            dma((4, 4)),
            dma,
            dma,
            pltpu.SemaphoreType.REGULAR,
            pltpu.SemaphoreType.REGULAR,
        ],
        compiler_params=pltpu.CompilerParams(
            collective_id=0, has_side_effects=True, vmem_limit_bytes=56 << 20
        ),
    )(
        slab,
        sample_counts,
        mode_rows_one,
        mode_rows_two,
        merge_tensor.reshape(96, 12, 8, 96),
        ancestral_modes,
    )


def solution(mesh):
    in_specs = (P("pop", "merge", None), P(), P(), P(), P(), P())
    out_specs = P(("pop", "merge"), None)
    return jax.shard_map(
        on_device, mesh=mesh, in_specs=in_specs, out_specs=out_specs, check_vma=False
    )
```

```python
import jax
import jax.numpy as jnp
from jax import lax
from jax.experimental import pallas as pl
from jax.experimental.pallas import tpu as pltpu
from jax.sharding import PartitionSpec as P

branch_one = 0.00025
branch_two = 0.0004
MESH = pl.DeviceIdType.MESH
HIGH = lax.Precision.HIGHEST
F32 = jnp.float32


def device(y, xh, z, xl, c):
    return ((y * 2 + xh) * 8 + z, xl * 2 + c)


def prepared(rows, count, branch):
    order = lax.broadcasted_iota(jnp.int32, rows.shape, 0).astype(F32)
    entry = lax.broadcasted_iota(jnp.int32, rows.shape, 1)
    decay = jnp.exp(-branch * order * (order + 1.0) / 2.0)
    return jnp.where(entry <= count, rows, 0.0) * decay


def kernel(
    slab, counts, rows_one, rows_two, merge, ancestral, out,
    slab_v, one_v, two_v, merge_v, anc_v, anc_pad, one_b, half_v, weights, whi, part, from_core,
    arrived_y, arrived_x, tiles_out, pieces, stack,
    load_sem, slab_sem, merge_sem, core_send, core_recv, y_send, y_recv, x_send, x_recv,
    final_send, final_recv, entered_near, entered_far,
):
    pop, mrg = lax.axis_index("pop"), lax.axis_index("merge")
    z = pop % 8
    xh = (pop // 8) % 2
    y = pop // 16
    xl, c = mrg // 2, mrg % 2
    zh = z // 2
    bits_yh, bits_yl = (y // 2, 1 - y // 2), (y % 2, 1 - y % 2)
    bits_xh, bits_xl = (xh, 1 - xh), (xl, 1 - xl)
    bits_zl, bits_c = (z % 2, 1 - z % 2), (c, 1 - c)
    ys = [bits_yh[k // 2] * 2 + bits_yl[k % 2] for k in range(4)]

    barrier = pltpu.get_barrier_semaphore()

    def tell(sem, dev):
        pl.semaphore_signal(sem, inc=1, device_id=dev, device_id_type=MESH)


    def y_target(i):
        return y, i % 4, bits_xh[1 - i // 4]

    def x_target(i):
        k = i % 4
        xr = 1 - k % 2
        u = (i // 4) * 2 + k // 2
        return u, u, xr

    def slab_copy(i, h):
        if h == 0:
            _, ty, tx = y_target(i)
            pair = ty * 4 + tx * 2
        else:
            _, ty, xr = x_target(i)
            pair = ty * 4 + bits_xh[xr] * 2 + 1
        begin = pl.multiple_of(pair * 256, 256)
        return pltpu.make_async_copy(
            slab.at[:, :, pl.ds(begin, 256)],
            slab_v.at[h * 2 + i // 4, :, :, pl.ds(i % 4 * 256, 256)],
            slab_sem.at[i, h],
        )

    load_one = pltpu.make_async_copy(rows_one, one_v, load_sem.at[0])
    load_two = pltpu.make_async_copy(rows_two, two_v, load_sem.at[1])
    load_anc = [
        pltpu.make_async_copy(
            ancestral.at[:, pl.ds(e * 128, 128)], anc_v.at[e], load_sem.at[2 + e]
        )
        for e in range(2)
    ]
    load_one.start()
    load_two.start()
    merge_loads = [
        pltpu.make_async_copy(
            merge.at[:, pl.ds(b * 4, 4)], merge_v.at[:, pl.ds(b * 4, 4)], merge_sem.at[b]
        )
        for b in range(3)
    ]
    for load in merge_loads:
        load.start()

    for k in (4, 3, 5, 2, 6, 1, 7):
        tell(barrier, device(y, xh, (z + k) % 8, xl, c))
    for k in (2, 3, 1):
        tell(barrier, device(ys[k], xh, z, xl, 1 - c))
        for core in range(2):
            tell(barrier, device(y, bits_xh[k // 2], z, bits_xl[k % 2], core))
    tell(barrier, device(y, xh, z, xl, 1 - c))
    for h in range(2):
        for i in range(8):
            slab_copy(i, h).start()
    for load in load_anc:
        load.start()
    own_piece = (z < 4) | (zh == 2 + xl)

    load_one.wait()
    load_two.wait()
    one = prepared(one_v[...], counts[0], branch_one)
    entry = lax.broadcasted_iota(jnp.int32, one.shape, 1)
    for a in range(4):
        column = jnp.sum(jnp.where(entry == pop * 4 + a, one, 0.0), axis=1, keepdims=True)
        one_b[a] = jnp.broadcast_to(column[:, :, None], (96, 8, 96))
    two = prepared(two_v[...], counts[1], branch_two)
    two = pltpu.roll(two, (256 - mrg * 64) % 256, 1)
    two_t = jnp.transpose(two[:, :128])[:64]
    two_hi = two_t.astype(jnp.bfloat16)
    two_lo = (two_t - two_hi.astype(F32)).astype(jnp.bfloat16)
    half_v[...] = jnp.zeros_like(half_v)
    for b in range(3):
        merge_loads[b].wait()

        def mode_step(mb, acc):
            for s in range(8):
                m = mb * 8 + s
                block = merge_v[m, b * 4 : b * 4 + 4]
                acc = tuple(acc[a] + one_b[a, m][None] * block for a in range(4))
            return acc

        acc = lax.fori_loop(0, 12, mode_step, tuple(jnp.zeros((4, 8, 96), F32) for _ in range(4)))
        for a in range(4):
            half_v[b * 32 : b * 32 + 32, a * 128 : a * 128 + 96] = acc[a].reshape(32, 96)
    half = half_v[...]
    half_hi = half.astype(jnp.bfloat16)
    half_lo = (half - half_hi.astype(F32)).astype(jnp.bfloat16)
    wide = (
        jnp.dot(two_hi, half_hi, preferred_element_type=F32)
        + jnp.dot(two_lo, half_hi, preferred_element_type=F32)
        + jnp.dot(two_hi, half_lo, preferred_element_type=F32)
    )
    flat = jnp.concatenate([wide[:, a * 128 : a * 128 + 128] for a in range(4)], axis=0)
    w = jnp.transpose(flat)[:96]
    w_hi = w.astype(jnp.bfloat16)
    weights[:96] = w_hi
    weights[96:] = (w - w_hi.astype(F32)).astype(jnp.bfloat16)
    whi[...] = w_hi

    def core_copy(i, h):
        return pltpu.make_async_remote_copy(
            src_ref=part.at[i, h, 1 - c],
            dst_ref=from_core.at[i, h],
            send_sem=core_send,
            recv_sem=core_recv.at[i, h],
            device_id=device(y, xh, z, xl, 1 - c),
            device_id_type=MESH,
        )

    def contract_pair(b, i):
        h, at = b // 2, b % 2 * 4 + i
        x = slab_v[b, :, :, i * 256 : i * 256 + 256].reshape(256, 256)
        x_hi = x.astype(jnp.bfloat16)
        x_lo = (x - x_hi.astype(F32)).astype(jnp.bfloat16)
        both = jnp.dot(weights[...], x_hi, preferred_element_type=F32)
        rest = jnp.dot(whi[...], x_lo, preferred_element_type=F32)
        total = both[:96] + both[96:] + rest
        for j in range(2):
            for t in range(2):
                part[at, h, j, t] = total[j * 48 : j * 48 + 48, t * 128 : t * 128 + 128]

    def arrive(b):
        for i in range(4):
            slab_copy(b % 2 * 4 + i, b // 2).wait()

    def contract(b):
        arrive(b)
        for i in range(4):
            contract_pair(b, i)

    def swap(b):
        for i in range(4):
            core_copy(b % 2 * 4 + i, b // 2).start()

    def settle(i, h):
        core_copy(i, h).wait_recv()
        part[i, h, c] = part[i, h, c] + from_core[i, h]

    def send_y(i, t):
        k, ty, _ = y_target(i)
        pltpu.make_async_remote_copy(
            src_ref=part.at[i, 0, c, t],
            dst_ref=arrived_y.at[k, i // 4, t],
            send_sem=y_send,
            recv_sem=y_recv.at[k, i // 4, t],
            device_id=device(ty, xh, z, xl, 1 - c),
            device_id_type=MESH,
        ).start()

    def send_x(i):
        u, _, xr = x_target(i)
        for tr in (1, 0):
            pltpu.make_async_remote_copy(
                src_ref=part.at[i, 1, c, bits_xl[tr]],
                dst_ref=arrived_x.at[xr * 2 + tr, u],
                send_sem=x_send,
                recv_sem=x_recv.at[xr * 2 + tr, u],
                device_id=device(y, bits_xh[xr], z, bits_xl[tr], 1 - c),
                device_id_type=MESH,
            ).start()

    arrive(0)
    contract_pair(0, 0)
    pl.semaphore_wait(barrier, 17)
    for core in range(2):
        tell(entered_near, device(y, xh, z, 1 - xl, core))
    for k in (2, 3):
        for core in range(2):
            tell(entered_far, device(y, 1 - xh, z, bits_xl[k % 2], core))
    core_copy(0, 0).start()
    for i in range(1, 4):
        contract_pair(0, i)
        core_copy(i, 0).start()
    contract(1)
    swap(1)
    for i in range(8):
        settle(i, 0)
        if i == 4:
            pl.semaphore_wait(entered_near, 2)
        send_y(i, 0)
    contract(2)
    swap(2)
    contract(3)
    swap(3)
    for i in range(4):
        settle(i, 1)
        send_x(i)
    for i in range(8):
        send_y(i, 1)
    for i in range(4, 8):
        settle(i, 1)
        send_x(i)
    pl.semaphore_wait(entered_far, 4)

    for load in load_anc:
        load.wait()
    anc_pad[...] = jnp.zeros_like(anc_pad)
    stack[...] = jnp.zeros_like(stack)
    for js in range(8):
        for half in range(2):
            at = js * 16 + half * 8
            for e in range(2):
                anc_pad[at : at + 6, e * 128 : e * 128 + 128] = anc_v[
                    e, pl.ds(half * 48 + js, 6, stride=8), :
                ]

    row = lax.broadcasted_iota(jnp.int32, (6, 8, 128), 1)
    group = lax.broadcasted_iota(jnp.int32, (6, 8, 128), 2) // 16

    def spread(total, n, h):
        x = total.reshape(6, 8, 128)
        for b in (1, 2, 4):
            odd_row, odd_group = row // b % 2 == 1, group // b % 2 == 1
            above = pltpu.roll(pltpu.roll(x, 8 - b, 1), 16 * b, 2)
            below = pltpu.roll(pltpu.roll(x, b, 1), 128 - 16 * b, 2)
            x = jnp.where(odd_row == odd_group, x, jnp.where(odd_group, above, below))
        for j in range(6):
            tiles_out[h, n, pl.ds(j, 8, stride=8), :] = x[j]

    def send_pieces(n, h, slot, ty, txh, tzh, own, gz):
        for r in range(4):
            gx, gc = bits_xl[r // 2], bits_c[r % 2]
            begin = pl.multiple_of(gz * 32 + gx * 16 + gc * 8, 8)
            send = pltpu.make_async_remote_copy(
                src_ref=tiles_out.at[h, n, pl.ds(begin, 6), :],
                dst_ref=pieces.at[slot, pl.ds(0, 6), :],
                send_sem=final_send,
                recv_sem=final_recv,
                device_id=device(ty, txh, tzh * 2 + gz, gx, gc),
                device_id_type=MESH,
            )
            if r == 0 and own is not None:
                mine = own & (z % 2 == gz)

                @pl.when(mine)
                def _():
                    pieces[slot, 0:6] = tiles_out[h, n, pl.ds(begin, 6), :]

                @pl.when(jnp.logical_not(mine))
                def _():
                    send.start()
            else:
                send.start()

    slot_y = (xh * 2 + xl) * 16 + z * 2 + c
    slot_x = y * 16 + z * 2 + c
    def deliver_y(n):
        q, t = n // 2, n % 2
        for k in range(4):
            pltpu.make_async_copy(
                arrived_y.at[k, q, t], arrived_y.at[k, q, t], y_recv.at[k, q, t]
            ).wait()
        spread(
            (arrived_y[0, q, t] + arrived_y[1, q, t]) + (arrived_y[2, q, t] + arrived_y[3, q, t]),
            n,
            0,
        )

    def send_z(n, gz):
        q, t = n // 2, n % 2
        send_pieces(n, 0, slot_y, y, bits_xh[1 - q], t, zh == t if q == 1 else None, gz)

    def deliver_x(n):
        q, t = n // 2, n % 2
        for k in range(4):
            pltpu.make_async_copy(
                arrived_x.at[k, n], arrived_x.at[k, n], x_recv.at[k, n]
            ).wait()
        spread((arrived_x[0, n] + arrived_x[1, n]) + (arrived_x[2, n] + arrived_x[3, n]), n, 1)
        for gz in (1, 0):
            send_pieces(n, 1, slot_x, n, xh, 2 + xl, (zh == 2 + xl) & (y == n), gz)

    deliver_y(0)
    send_z(0, 0)
    send_z(0, 1)
    deliver_y(2)
    send_z(2, 0)
    send_z(2, 1)
    deliver_y(1)
    send_z(1, 1)
    send_z(1, 0)
    deliver_y(3)
    send_z(3, 1)
    send_z(3, 0)
    deliver_x(0)
    deliver_x(1)
    deliver_x(2)
    deliver_x(3)

    def drain(ref, sem):
        pltpu.make_async_copy(ref, ref, sem).wait()

    def drain_pieces(sem):
        @pl.when(own_piece)
        def _():
            drain(pieces.at[pl.ds(0, 63), pl.ds(0, 6), :], sem)

        @pl.when(jnp.logical_not(own_piece))
        def _():
            drain(pieces.at[:, pl.ds(0, 6), :], sem)

    drain_pieces(final_recv)

    upper, lower = pieces[0, 0:6], pieces[1, 0:6]
    for i in range(1, 32):
        upper = upper + pieces[i * 2, 0:6]
        lower = lower + pieces[i * 2 + 1, 0:6]
    stack[0:6] = lower
    stack[8:14] = upper
    turned = jnp.transpose(stack[...])
    left = turned[0:16]
    for js in range(1, 8):
        left = left + pltpu.roll(turned[js * 16 : js * 16 + 16], js * 16, 1)
    out[...] = jnp.dot(left, anc_pad[...], precision=HIGH, preferred_element_type=F32)

    drain(from_core, core_send)
    drain(arrived_y, y_send)
    drain(arrived_x, x_send)
    drain_pieces(final_send)


def on_device(slab, sample_counts, mode_rows_one, mode_rows_two, merge_tensor, ancestral_modes):
    hbm = pl.BlockSpec(memory_space=pl.ANY)
    dma = pltpu.SemaphoreType.DMA
    return pl.pallas_call(
        kernel,
        out_shape=pltpu.VMEM((16, 256), F32),
        in_specs=[hbm, pl.BlockSpec(memory_space=pltpu.SMEM), hbm, hbm, hbm, hbm],
        out_specs=pl.BlockSpec(memory_space=pltpu.VMEM),
        scratch_shapes=[
            pltpu.VMEM((4, 4, 64, 1024), F32),
            pltpu.VMEM((96, 256), F32),
            pltpu.VMEM((96, 256), F32),
            pltpu.VMEM((96, 12, 8, 96), F32),
            pltpu.VMEM((2, 96, 128), F32),
            pltpu.VMEM((128, 256), F32),
            pltpu.VMEM((4, 96, 8, 96), F32),
            pltpu.VMEM((96, 512), F32),
            pltpu.VMEM((192, 256), jnp.bfloat16),
            pltpu.VMEM((96, 256), jnp.bfloat16),
            pltpu.VMEM((8, 2, 2, 2, 48, 128), F32),
            pltpu.VMEM((8, 2, 2, 48, 128), F32),
            pltpu.VMEM((4, 2, 2, 48, 128), F32),
            pltpu.VMEM((4, 4, 48, 128), F32),
            pltpu.VMEM((2, 4, 64, 128), F32),
            pltpu.VMEM((64, 8, 128), F32),
            pltpu.VMEM((128, 128), F32),
            dma((4,)),
            dma((8, 2)),
            dma((3,)),
            dma,
            dma((8, 2)),
            dma,
            dma((4, 2, 2)),
            dma,
            dma((4, 4)),
            dma,
            dma,
            pltpu.SemaphoreType.REGULAR,
            pltpu.SemaphoreType.REGULAR,
        ],
        compiler_params=pltpu.CompilerParams(
            collective_id=0, has_side_effects=True, vmem_limit_bytes=56 << 20
        ),
    )(
        slab,
        sample_counts,
        mode_rows_one,
        mode_rows_two,
        merge_tensor.reshape(96, 12, 8, 96),
        ancestral_modes,
    )


def solution(mesh):
    in_specs = (P("pop", "merge", None), P(), P(), P(), P(), P())
    out_specs = P(("pop", "merge"), None)
    return jax.shard_map(
        on_device, mesh=mesh, in_specs=in_specs, out_specs=out_specs, check_vma=False
    )
```

```python
import jax
import jax.numpy as jnp
from jax import lax
from jax.experimental import pallas as pl
from jax.experimental.pallas import tpu as pltpu
from jax.sharding import PartitionSpec as P

branch_one = 0.00025
branch_two = 0.0004
MESH = pl.DeviceIdType.MESH
HIGH = lax.Precision.HIGHEST
F32 = jnp.float32


def device(y, xh, z, xl, c):
    return ((y * 2 + xh) * 8 + z, xl * 2 + c)


def prepared(rows, count, branch):
    order = lax.broadcasted_iota(jnp.int32, rows.shape, 0).astype(F32)
    entry = lax.broadcasted_iota(jnp.int32, rows.shape, 1)
    decay = jnp.exp(-branch * order * (order + 1.0) / 2.0)
    return jnp.where(entry <= count, rows, 0.0) * decay


def kernel(
    slab, counts, rows_one, rows_two, merge, ancestral, out,
    slab_v, one_v, two_v, merge_v, anc_v, anc_pad, one_b, half_v, weights, whi, part, from_core,
    arrived_y, arrived_x, tiles_out, pieces, stack,
    load_sem, slab_sem, merge_sem, core_send, core_recv, y_send, y_recv, x_send, x_recv,
    final_send, final_recv, entered_near, entered_far,
):
    pop, mrg = lax.axis_index("pop"), lax.axis_index("merge")
    z = pop % 8
    xh = (pop // 8) % 2
    y = pop // 16
    xl, c = mrg // 2, mrg % 2
    zh = z // 2
    bits_yh, bits_yl = (y // 2, 1 - y // 2), (y % 2, 1 - y % 2)
    bits_xh, bits_xl = (xh, 1 - xh), (xl, 1 - xl)
    bits_zl, bits_c = (z % 2, 1 - z % 2), (c, 1 - c)
    ys = [bits_yh[k // 2] * 2 + bits_yl[k % 2] for k in range(4)]

    barrier = pltpu.get_barrier_semaphore()

    def tell(sem, dev):
        pl.semaphore_signal(sem, inc=1, device_id=dev, device_id_type=MESH)


    def y_target(i):
        return y, i % 4, bits_xh[1 - i // 4]

    def x_target(i):
        k = i % 4
        xr = 1 - k % 2
        u = (i // 4) * 2 + k // 2
        return u, u, xr

    def slab_copy(i, h):
        if h == 0:
            _, ty, tx = y_target(i)
            pair = ty * 4 + tx * 2
        else:
            _, ty, xr = x_target(i)
            pair = ty * 4 + bits_xh[xr] * 2 + 1
        begin = pl.multiple_of(pair * 256, 256)
        return pltpu.make_async_copy(
            slab.at[:, :, pl.ds(begin, 256)],
            slab_v.at[h * 2 + i // 4, :, :, pl.ds(i % 4 * 256, 256)],
            slab_sem.at[i, h],
        )

    load_one = pltpu.make_async_copy(rows_one, one_v, load_sem.at[0])
    load_two = pltpu.make_async_copy(rows_two, two_v, load_sem.at[1])
    load_anc = [
        pltpu.make_async_copy(
            ancestral.at[:, pl.ds(e * 128, 128)], anc_v.at[e], load_sem.at[2 + e]
        )
        for e in range(2)
    ]
    load_one.start()
    load_two.start()
    merge_loads = [
        pltpu.make_async_copy(
            merge.at[:, pl.ds(b * 4, 4)], merge_v.at[:, pl.ds(b * 4, 4)], merge_sem.at[b]
        )
        for b in range(3)
    ]
    for load in merge_loads:
        load.start()

    for k in (4, 3, 5, 2, 6, 1, 7):
        tell(barrier, device(y, xh, (z + k) % 8, xl, c))
    for k in (2, 3, 1):
        tell(barrier, device(ys[k], xh, z, xl, 1 - c))
        for core in range(2):
            tell(barrier, device(y, bits_xh[k // 2], z, bits_xl[k % 2], core))
    tell(barrier, device(y, xh, z, xl, 1 - c))
    for h in range(2):
        for i in range(8):
            slab_copy(i, h).start()
    for load in load_anc:
        load.start()
    own_piece = (z < 4) | (zh == 2 + xl)

    load_one.wait()
    load_two.wait()
    one = prepared(one_v[...], counts[0], branch_one)
    entry = lax.broadcasted_iota(jnp.int32, one.shape, 1)
    for a in range(4):
        column = jnp.sum(jnp.where(entry == pop * 4 + a, one, 0.0), axis=1, keepdims=True)
        one_b[a] = jnp.broadcast_to(column[:, :, None], (96, 8, 96))
    two = prepared(two_v[...], counts[1], branch_two)
    two = pltpu.roll(two, (256 - mrg * 64) % 256, 1)
    two_t = jnp.transpose(two[:, :128])[:64]
    two_hi = two_t.astype(jnp.bfloat16)
    two_lo = (two_t - two_hi.astype(F32)).astype(jnp.bfloat16)
    half_v[...] = jnp.zeros_like(half_v)
    for b in range(3):
        merge_loads[b].wait()

        def mode_step(mb, acc):
            for s in range(8):
                m = mb * 8 + s
                block = merge_v[m, b * 4 : b * 4 + 4]
                acc = tuple(acc[a] + one_b[a, m][None] * block for a in range(4))
            return acc

        acc = lax.fori_loop(0, 12, mode_step, tuple(jnp.zeros((4, 8, 96), F32) for _ in range(4)))
        for a in range(4):
            half_v[b * 32 : b * 32 + 32, a * 128 : a * 128 + 96] = acc[a].reshape(32, 96)
    half = half_v[...]
    half_hi = half.astype(jnp.bfloat16)
    half_lo = (half - half_hi.astype(F32)).astype(jnp.bfloat16)
    wide = (
        jnp.dot(two_hi, half_hi, preferred_element_type=F32)
        + jnp.dot(two_lo, half_hi, preferred_element_type=F32)
        + jnp.dot(two_hi, half_lo, preferred_element_type=F32)
    )
    flat = jnp.concatenate([wide[:, a * 128 : a * 128 + 128] for a in range(4)], axis=0)
    w = jnp.transpose(flat)[:96]
    w_hi = w.astype(jnp.bfloat16)
    weights[:96] = w_hi
    weights[96:] = (w - w_hi.astype(F32)).astype(jnp.bfloat16)
    whi[...] = w_hi

    def core_copy(i, h):
        return pltpu.make_async_remote_copy(
            src_ref=part.at[i, h, 1 - c],
            dst_ref=from_core.at[i, h],
            send_sem=core_send,
            recv_sem=core_recv.at[i, h],
            device_id=device(y, xh, z, xl, 1 - c),
            device_id_type=MESH,
        )

    def contract_pair(b, i):
        h, at = b // 2, b % 2 * 4 + i
        x = slab_v[b, :, :, i * 256 : i * 256 + 256].reshape(256, 256)
        x_hi = x.astype(jnp.bfloat16)
        x_lo = (x - x_hi.astype(F32)).astype(jnp.bfloat16)
        both = jnp.dot(weights[...], x_hi, preferred_element_type=F32)
        rest = jnp.dot(whi[...], x_lo, preferred_element_type=F32)
        total = both[:96] + both[96:] + rest
        for j in range(2):
            for t in range(2):
                part[at, h, j, t] = total[j * 48 : j * 48 + 48, t * 128 : t * 128 + 128]

    def arrive(b):
        for i in range(4):
            slab_copy(b % 2 * 4 + i, b // 2).wait()

    def contract(b):
        arrive(b)
        for i in range(4):
            contract_pair(b, i)

    def swap(b):
        for i in range(4):
            core_copy(b % 2 * 4 + i, b // 2).start()

    def settle(i, h):
        core_copy(i, h).wait_recv()
        part[i, h, c] = part[i, h, c] + from_core[i, h]

    def send_y(i, t):
        k, ty, _ = y_target(i)
        pltpu.make_async_remote_copy(
            src_ref=part.at[i, 0, c, t],
            dst_ref=arrived_y.at[k, i // 4, t],
            send_sem=y_send,
            recv_sem=y_recv.at[k, i // 4, t],
            device_id=device(ty, xh, z, xl, 1 - c),
            device_id_type=MESH,
        ).start()

    def send_x(i):
        u, _, xr = x_target(i)
        for tr in (1, 0):
            pltpu.make_async_remote_copy(
                src_ref=part.at[i, 1, c, bits_xl[tr]],
                dst_ref=arrived_x.at[xr * 2 + tr, u],
                send_sem=x_send,
                recv_sem=x_recv.at[xr * 2 + tr, u],
                device_id=device(y, bits_xh[xr], z, bits_xl[tr], 1 - c),
                device_id_type=MESH,
            ).start()

    arrive(0)
    contract_pair(0, 0)
    pl.semaphore_wait(barrier, 17)
    for core in range(2):
        tell(entered_near, device(y, xh, z, 1 - xl, core))
    for k in (2, 3):
        for core in range(2):
            tell(entered_far, device(y, 1 - xh, z, bits_xl[k % 2], core))
    core_copy(0, 0).start()
    for i in range(1, 4):
        contract_pair(0, i)
        core_copy(i, 0).start()
    contract(1)
    swap(1)
    for i in range(8):
        settle(i, 0)
        if i == 4:
            pl.semaphore_wait(entered_near, 2)
        send_y(i, 0)
    for i in range(8):
        send_y(i, 1)
    contract(2)
    swap(2)
    contract(3)
    swap(3)
    for i in range(4):
        settle(i, 1)
        send_x(i)
    for i in range(4, 8):
        settle(i, 1)
        send_x(i)
    pl.semaphore_wait(entered_far, 4)

    for load in load_anc:
        load.wait()
    anc_pad[...] = jnp.zeros_like(anc_pad)
    stack[...] = jnp.zeros_like(stack)
    for js in range(8):
        for half in range(2):
            at = js * 16 + half * 8
            for e in range(2):
                anc_pad[at : at + 6, e * 128 : e * 128 + 128] = anc_v[
                    e, pl.ds(half * 48 + js, 6, stride=8), :
                ]

    row = lax.broadcasted_iota(jnp.int32, (6, 8, 128), 1)
    group = lax.broadcasted_iota(jnp.int32, (6, 8, 128), 2) // 16

    def spread(total, n, h):
        x = total.reshape(6, 8, 128)
        for b in (1, 2, 4):
            odd_row, odd_group = row // b % 2 == 1, group // b % 2 == 1
            above = pltpu.roll(pltpu.roll(x, 8 - b, 1), 16 * b, 2)
            below = pltpu.roll(pltpu.roll(x, b, 1), 128 - 16 * b, 2)
            x = jnp.where(odd_row == odd_group, x, jnp.where(odd_group, above, below))
        for j in range(6):
            tiles_out[h, n, pl.ds(j, 8, stride=8), :] = x[j]

    def send_pieces(n, h, slot, ty, txh, tzh, own, near):
        for r in range(8):
            gz, gx, gc = near + r // 4 * (1 - 2 * near), bits_xl[r // 2 % 2], bits_c[r % 2]
            begin = pl.multiple_of(gz * 32 + gx * 16 + gc * 8, 8)
            send = pltpu.make_async_remote_copy(
                src_ref=tiles_out.at[h, n, pl.ds(begin, 6), :],
                dst_ref=pieces.at[slot, pl.ds(0, 6), :],
                send_sem=final_send,
                recv_sem=final_recv,
                device_id=device(ty, txh, tzh * 2 + gz, gx, gc),
                device_id_type=MESH,
            )
            if r % 4 == 0 and own is not None:
                mine = own & (z % 2 == gz)

                @pl.when(mine)
                def _():
                    pieces[slot, 0:6] = tiles_out[h, n, pl.ds(begin, 6), :]

                @pl.when(jnp.logical_not(mine))
                def _():
                    send.start()
            else:
                send.start()

    slot_y = (xh * 2 + xl) * 16 + z * 2 + c
    slot_x = y * 16 + z * 2 + c
    def deliver_y(n):
        q, t = n // 2, n % 2
        for k in range(4):
            pltpu.make_async_copy(
                arrived_y.at[k, q, t], arrived_y.at[k, q, t], y_recv.at[k, q, t]
            ).wait()
        spread(
            (arrived_y[0, q, t] + arrived_y[1, q, t]) + (arrived_y[2, q, t] + arrived_y[3, q, t]),
            n,
            0,
        )
        send_pieces(n, 0, slot_y, y, bits_xh[1 - q], t, zh == t if q == 1 else None, t)

    def deliver_x(n):
        q, t = n // 2, n % 2
        for k in range(4):
            pltpu.make_async_copy(
                arrived_x.at[k, n], arrived_x.at[k, n], x_recv.at[k, n]
            ).wait()
        spread((arrived_x[0, n] + arrived_x[1, n]) + (arrived_x[2, n] + arrived_x[3, n]), n, 1)
        send_pieces(n, 1, slot_x, n, xh, 2 + xl, (zh == 2 + xl) & (y == n), 0)

    deliver_y(0)
    deliver_y(2)
    deliver_y(1)
    deliver_y(3)
    deliver_x(0)
    deliver_x(1)
    deliver_x(2)
    deliver_x(3)

    def drain(ref, sem):
        pltpu.make_async_copy(ref, ref, sem).wait()

    def drain_pieces(sem):
        @pl.when(own_piece)
        def _():
            drain(pieces.at[pl.ds(0, 63), pl.ds(0, 6), :], sem)

        @pl.when(jnp.logical_not(own_piece))
        def _():
            drain(pieces.at[:, pl.ds(0, 6), :], sem)

    drain_pieces(final_recv)

    upper, lower = pieces[0, 0:6], pieces[1, 0:6]
    for i in range(1, 32):
        upper = upper + pieces[i * 2, 0:6]
        lower = lower + pieces[i * 2 + 1, 0:6]
    stack[0:6] = lower
    stack[8:14] = upper
    turned = jnp.transpose(stack[...])
    left = turned[0:16]
    for js in range(1, 8):
        left = left + pltpu.roll(turned[js * 16 : js * 16 + 16], js * 16, 1)
    out[...] = jnp.dot(left, anc_pad[...], precision=HIGH, preferred_element_type=F32)

    drain(from_core, core_send)
    drain(arrived_y, y_send)
    drain(arrived_x, x_send)
    drain_pieces(final_send)


def on_device(slab, sample_counts, mode_rows_one, mode_rows_two, merge_tensor, ancestral_modes):
    hbm = pl.BlockSpec(memory_space=pl.ANY)
    dma = pltpu.SemaphoreType.DMA
    return pl.pallas_call(
        kernel,
        out_shape=pltpu.VMEM((16, 256), F32),
        in_specs=[hbm, pl.BlockSpec(memory_space=pltpu.SMEM), hbm, hbm, hbm, hbm],
        out_specs=pl.BlockSpec(memory_space=pltpu.VMEM),
        scratch_shapes=[
            pltpu.VMEM((4, 4, 64, 1024), F32),
            pltpu.VMEM((96, 256), F32),
            pltpu.VMEM((96, 256), F32),
            pltpu.VMEM((96, 12, 8, 96), F32),
            pltpu.VMEM((2, 96, 128), F32),
            pltpu.VMEM((128, 256), F32),
            pltpu.VMEM((4, 96, 8, 96), F32),
            pltpu.VMEM((96, 512), F32),
            pltpu.VMEM((192, 256), jnp.bfloat16),
            pltpu.VMEM((96, 256), jnp.bfloat16),
            pltpu.VMEM((8, 2, 2, 2, 48, 128), F32),
            pltpu.VMEM((8, 2, 2, 48, 128), F32),
            pltpu.VMEM((4, 2, 2, 48, 128), F32),
            pltpu.VMEM((4, 4, 48, 128), F32),
            pltpu.VMEM((2, 4, 64, 128), F32),
            pltpu.VMEM((64, 8, 128), F32),
            pltpu.VMEM((128, 128), F32),
            dma((4,)),
            dma((8, 2)),
            dma((3,)),
            dma,
            dma((8, 2)),
            dma,
            dma((4, 2, 2)),
            dma,
            dma((4, 4)),
            dma,
            dma,
            pltpu.SemaphoreType.REGULAR,
            pltpu.SemaphoreType.REGULAR,
        ],
        compiler_params=pltpu.CompilerParams(
            collective_id=0, has_side_effects=True, vmem_limit_bytes=56 << 20
        ),
    )(
        slab,
        sample_counts,
        mode_rows_one,
        mode_rows_two,
        merge_tensor.reshape(96, 12, 8, 96),
        ancestral_modes,
    )


def solution(mesh):
    in_specs = (P("pop", "merge", None), P(), P(), P(), P(), P())
    out_specs = P(("pop", "merge"), None)
    return jax.shard_map(
        on_device, mesh=mesh, in_specs=in_specs, out_specs=out_specs, check_vma=False
    )
```
